32 devices in a mesh: gy: 8 (over y, x, core), gz: 4 (over z).
Axes of the slice: x: 2, y: 2, z: 4, core: 2. Of those that a mesh axis runs over, the one named last changes fastest.
Arguments:
- template: float32 [16, 128, 512], P('gz', 'gy'), may hold values from -4 to 4
- target_image: float32 [16, 128, 512], P('gz', 'gy'), may hold values from -4 to 4
- departure_shifts: int32 [4, 3, 16, 128, 512], P(None, None, 'gz', 'gy'), may hold values from -2 to 1
- departure_fractions: float32 [4, 3], replicated, may hold values from 0.1 to 0.9
Outputs:
- update: float32 [3, 16, 128, 512], P(None, 'gz', 'gy')
- deformed: float32 [16, 128, 512], P('gz', 'gy')
The draws below stay inside these ranges and needn't reach their ends.
All inputs are finite; a program needn't handle non-finite values.
Results may differ from the reference program's by a relative error of at most 0.00029.
Values sent between devices are 32-bit elements; how exact they have to be, the bound alone decides.
A program may use at most 128 MiB of HBM per device.

```python
import jax
import jax.numpy as jnp
from jax import lax

NX = 512
STEPS = 4
CHEB = 8
NY = 128
NZ = 16


def draw_template(key, part):
    rough = jnp.clip(jax.random.normal(key, (NZ, NY, NX), jnp.float32), -4.0, 4.0)
    return rough


def with_ends(values, stream_key, least, high):
    spot = [jax.random.randint(jax.random.fold_in(stream_key, axis), (), 0, length) for axis, length in enumerate(values.shape)]
    longest = values.shape.index(max(values.shape))
    neighbour = spot[:longest] + [(spot[longest] + 1) % values.shape[longest]] + spot[longest + 1:]
    return values.at[tuple(spot)].set(least).at[tuple(neighbour)].set(high)


def levels(rng, shape, shards, smallest, largest):
    factor_of, own = 1.0, jax.random.fold_in(rng, 6)
    for dim, shards_of in shards:
        heights = jnp.exp(jax.random.uniform(jax.random.fold_in(own, dim), (shards_of,), jnp.float32, smallest / len(shards), largest / len(shards)))
        factor_of = factor_of * jnp.repeat(heights, shape[dim] // shards_of).reshape([-1 if axis == dim else 1 for axis in range(len(shape))])
    return factor_of


def centred(key, shape, scale, limit, split=(), held_as=jnp.bfloat16):
    array = jax.random.normal(key, shape, jnp.float32) * scale
    if len(split) > 0:
        array = levels(key, shape, split, -0.22, 0.18) * array
    return jnp.clip(array, min=-limit, max=limit).astype(held_as)


def setup_inputs(seed: int = 0) -> dict:
    key_of = jax.random.split(jax.random.key(seed), 5)
    return {
        "template": draw_template(jax.random.fold_in(key_of[4], 71), 0),
        "target_image": centred(key_of[1], (NZ, NY, NX), 1.0, 4.0, ((0, 4), (1, 8)), jnp.float32),
        "departure_shifts": with_ends(jax.random.randint(key_of[2], (STEPS, 3, NZ, NY, NX), -2, 2), jax.random.fold_in(key_of[2], 1), -2, 1).astype(jnp.int32),
        "departure_fractions": jnp.clip(jax.random.uniform(key_of[3], (STEPS, 3), jnp.float32, 0.1, 0.9), 0.1, 0.9),
    }


DAMPING = 0.25
ACROSS_WEIGHT = 0.0625
ALONG_SCALE = 32.0
SHIFT = 0.25


def cubic_weights(fraction):
    return (-fraction * (fraction - 1.0) * (fraction - 2.0) / 6.0,
            (fraction + 1.0) * (fraction - 1.0) * (fraction - 2.0) / 2.0,
            -(fraction + 1.0) * fraction * (fraction - 2.0) / 2.0,
            (fraction + 1.0) * fraction * (fraction - 1.0) / 6.0)


def advect_axis(field, shifts, fraction, axis):
    weights = cubic_weights(fraction)
    filtered = weights[0] * jnp.roll(field, 1, axis)
    for node in range(1, 4):
        filtered = filtered + weights[node] * jnp.roll(field, 1 - node, axis)
    result = jnp.roll(filtered, -1, axis)
    for offset in (0, -1, -2):
        result = jnp.where(shifts == offset, jnp.roll(filtered, -offset, axis), result)
    return result


def spectral_gain(length_y, freq_x, length_x):
    freq_y = jnp.arange(length_y).astype(jnp.float32)
    sine_y = jnp.sin(jnp.pi * freq_y / length_y) ** 2
    sine_x = jnp.sin(jnp.pi * freq_x.astype(jnp.float32) / length_x) ** 2
    weight_y = (length_y / ALONG_SCALE) ** 2
    return 1.0 / (DAMPING + 4.0 * (weight_y * sine_y[:, None] + ACROSS_WEIGHT * sine_x[None, :]))


def operate_coarse(field):
    beside = jnp.roll(field, -1, 1) + jnp.roll(field, 1, 1)
    beside = beside + jnp.roll(field, -1, 2) + jnp.roll(field, 1, 2)
    beside = beside + jnp.roll(field, -1, 3) + jnp.roll(field, 1, 3)
    return (SHIFT + 6.0) * field - beside


def chebyshev(rhs, operate, count):
    low = SHIFT
    high = SHIFT + 12.0
    theta = (high + low) / 2.0
    delta = (high - low) / 2.0
    sigma = theta / delta
    ratio_now = 1.0 / sigma
    residual = rhs
    direction = rhs / theta
    solution = jnp.zeros_like(rhs)
    for turn in range(count):
        solution = solution + direction
        if turn + 1 < count:
            residual = residual - operate(direction)
            ratio_next = 1.0 / (2.0 * sigma - ratio_now)
            direction = (ratio_next * ratio_now) * direction + (2.0 * ratio_next / delta) * residual
            ratio_now = ratio_next
    return solution


def reference(template, target_image, departure_shifts, departure_fractions):
    image = template
    for step in range(STEPS):
        image = advect_axis(image, departure_shifts[step, 0], departure_fractions[step, 0], 2)
        image = advect_axis(image, departure_shifts[step, 1], departure_fractions[step, 1], 1)
        image = advect_axis(image, departure_shifts[step, 2], departure_fractions[step, 2], 0)
    grad_x = (jnp.roll(image, -1, 2) - jnp.roll(image, 1, 2)) * 0.5
    grad_y = (jnp.roll(image, -1, 1) - jnp.roll(image, 1, 1)) * 0.5
    grad_z = (jnp.roll(image, -1, 0) - jnp.roll(image, 1, 0)) * 0.5
    mismatch = image - target_image
    forces = jnp.stack([mismatch * grad_x, mismatch * grad_y, mismatch * grad_z])
    gain = spectral_gain(NY, jnp.arange(NX), NX)

    def smooth_one(force):
        spectrum = jnp.fft.fft2(force, axes=(1, 2))
        return jnp.real(jnp.fft.ifft2(spectrum * gain, axes=(1, 2))).astype(force.dtype)

    smooth = lax.map(smooth_one, forces)
    coarse = forces.reshape(3, NZ // 2, 2, NY // 2, 2, NX // 2, 2).mean(axis=(2, 4, 6))
    solved = chebyshev(coarse, operate_coarse, CHEB)
    fine = jnp.repeat(jnp.repeat(jnp.repeat(solved, 2, 1), 2, 2), 2, 3)
    update = -(smooth + fine)
    return update, image
```

```python
import functools

import jax
import jax.numpy as jnp
import numpy as np
from jax import lax
from jax.experimental import pallas as pl
from jax.experimental.pallas import tpu as pltpu
from jax.sharding import PartitionSpec as P

CHEB = 8
DAMPING = 0.25
ACROSS_WEIGHT = 0.0625
ALONG_SCALE = 32.0
SHIFT = 0.25
MESH = pl.DeviceIdType.MESH
EDGE = 4
HALO = 3


def cubic_weights(fraction):
    return (
        -fraction * (fraction - 1.0) * (fraction - 2.0) / 6.0,
        (fraction + 1.0) * (fraction - 1.0) * (fraction - 2.0) / 2.0,
        -(fraction + 1.0) * fraction * (fraction - 2.0) / 2.0,
        (fraction + 1.0) * fraction * (fraction - 1.0) / 6.0,
    )


def turn_factors(count):
    low, high = SHIFT, SHIFT + 12.0
    theta, delta = (high + low) / 2.0, (high - low) / 2.0
    sigma = theta / delta
    now = 1.0 / sigma
    factors = []
    for _ in range(count - 1):
        after = 1.0 / (2.0 * sigma - now)
        factors.append((after * now, 2.0 * after / delta))
        now = after
    return theta, factors


def make_tables(rows, length_x, peers):
    length_y = rows * peers
    index = np.arange(length_x)
    angle = 2.0 * np.pi / length_x * (np.outer(index, index) % length_x)
    hartley = np.cos(angle) + np.sin(angle)
    weight = (length_y / ALONG_SCALE) ** 2
    a = DAMPING + 4.0 * ACROSS_WEIGHT * np.sin(np.pi * index / length_x) ** 2
    half = a / (2.0 * weight)
    r = 1.0 / (1.0 + half + np.sqrt(half * (half + 2.0)))
    y = np.arange(rows)[:, None]
    scale = 1.0 / (weight * (1.0 / r - r) * length_x)
    down, up, stride = [], [], 1
    while stride < rows:
        down.append(np.where(y >= stride, r ** stride, 0.0))
        up.append(np.where(y < rows - stride, r ** stride, 0.0))
        stride *= 2
    tables = [r ** (rows - 1 - y), r ** y, scale * r ** (y + 1), scale * r ** (rows - y),
              scale + 0.0 * r * y] + down + up
    m = np.arange(peers)[:, None]
    hops = r ** (rows * m) / (1.0 - r ** length_y)
    high = hartley.astype(jnp.bfloat16)
    low = (hartley - high.astype(np.float64)).astype(jnp.bfloat16)
    return high, low, np.stack(tables).astype(np.float32), hops.astype(np.float32)


def dot3(high, low, table_high, table_low):
    f = functools.partial(jnp.dot, preferred_element_type=jnp.float32)
    return f(high, table_high) + (f(low, table_high) + f(high, table_low))


def split(value):
    high = value.astype(jnp.bfloat16)
    return high, (value - high.astype(jnp.float32)).astype(jnp.bfloat16)


def choose(shift, options):
    minus2, minus1, zero, one = options
    result = jnp.where(shift == 0, zero, one)
    result = jnp.where(shift == -1, minus1, result)
    return jnp.where(shift == -2, minus2, result)


def kernel(ny, nz, fractions, *refs):
    count = 11
    sources, (update, deformed), rest = refs[:count], refs[count:count + 2], refs[count + 2:]
    held, fetch_sems, shift_sems = rest[:count], rest[count], rest[count + 1]
    step_count = held[2].shape[0]
    fetches = {}
    for i in (0, 1, 3, 4, 5, 6, 7, 8, 9, 10):
        fetches[i] = pltpu.make_async_copy(sources[i], held[i], fetch_sems.at[i])

    def fetch_shifts(step):
        return pltpu.make_async_copy(sources[2].at[step], held[2].at[step], shift_sems.at[step])

    fetches[0].start()
    for step in range(step_count):
        fetch_shifts(step).start()
    for i in (1, 7, 9, 3, 4, 5, 6, 8, 10):
        fetches[i].start()
    body(ny, nz, fractions, fetches, fetch_shifts, *held, update, deformed, *rest[count + 2:])


def body(ny, nz, fractions, fetches, fetch_shifts, template, target, shifts, hart_hi, hart_lo,
         tables, hops, pair_x, spread_x, pair_y, spread_y, update, deformed, img, ypad, yf, ysend, yrecv, zmid, zrecv, zmid_edge, zrecv_edge,
           zf, grecv, forces, ghat, msend, mrecv, coarse, left, right, dir_a, dir_b, resid, solved,
           zsum, fhi, flo, ys_send, ys_recv, zs_send, zs_recv, gs_send, gs_recv, ms_send, ms_recv,
           cs_send, cs_recv, hs_send, hs_recv):
    depth, rows, width = template.shape
    steps = shifts.shape[0]
    cz = 3 * depth
    me_y, me_z = lax.axis_index("gy"), lax.axis_index("gz")

    def at_y(offset):
        return (lax.rem(me_y + (offset + ny), ny), me_z)

    def at_z(offset):
        return (me_y, lax.rem(me_z + (offset + nz), nz))

    def copy(src, dst, send, recv, device):
        return pltpu.make_async_remote_copy(
            src_ref=src, dst_ref=dst, send_sem=send, recv_sem=recv, device_id=device,
            device_id_type=MESH)

    barrier = pltpu.get_barrier_semaphore()
    for d in range(1, ny):
        pl.semaphore_signal(barrier, inc=1, device_id=at_y(d), device_id_type=MESH)
    for d in range(1, nz):
        pl.semaphore_signal(barrier, inc=1, device_id=at_z(d), device_id_type=MESH)

    def rolled(value, by, axis):
        return pltpu.roll(value, by % value.shape[axis], axis)

    fetches[0].wait()
    for z in range(depth):
        img[z] = template[z]
    pl.semaphore_wait(barrier, ny + nz - 2)

    chunks = depth * EDGE // 8
    per = depth // chunks

    def y_copies(step, chunk):
        part = pl.ds(chunk * 8, 8)
        return [copy(ysend.at[step, side, part], yrecv.at[step, side, part],
                     ys_send.at[step, side, chunk], ys_recv.at[step, side, chunk],
                     at_y(1 - 2 * side)) for side in range(2)]

    inner = (((EDGE, rows - 2 * EDGE, 0),), zmid, zrecv, 0)
    outer = (((0, EDGE, 0), (rows - EDGE, EDGE, EDGE)), zmid_edge, zrecv_edge, 1)

    def z_copies(step, part):
        _, mid, received, which = part
        return [copy(mid.at[step, pl.ds(0 if side else depth - HALO, HALO)],
                     received.at[step, side], zs_send.at[step, side, which],
                     zs_recv.at[step, side, which], at_z(1 - 2 * side)) for side in range(2)]

    def put_edges(step, z, value):
        ypad[z, pl.ds(8, rows), :] = value
        ysend[step, 0, pl.ds(z * EDGE, EDGE), :] = value[rows - EDGE:, :]
        ysend[step, 1, pl.ds(z * EDGE, EDGE), :] = value[:EDGE, :]

    def take_edges(step, z):
        ypad[z, pl.ds(8 - EDGE, EDGE), :] = yrecv[step, 0, pl.ds(z * EDGE, EDGE), :]
        ypad[z, pl.ds(8 + rows, EDGE), :] = yrecv[step, 1, pl.ds(z * EDGE, EDGE), :]

    def advance(step, carry):
        fetch_shifts(step).wait()
        w = cubic_weights(fractions[step, 0])

        def pass_x(u, shift):
            f = (w[0] * rolled(u, 1, 1) + w[1] * u + w[2] * rolled(u, -1, 1)
                 + w[3] * rolled(u, -2, 1))
            return choose(shift, (rolled(f, 2, 1), rolled(f, 1, 1), f, rolled(f, -1, 1)))

        first, last = pl.ds(0, EDGE), pl.ds(rows - EDGE, EDGE)
        for z in range(depth):
            value = pass_x(
                jnp.concatenate([img[z, first, :], img[z, last, :]], axis=0),
                jnp.concatenate([shifts[step, 0, z, first, :], shifts[step, 0, z, last, :]],
                                axis=0))
            ypad[z, pl.ds(8, EDGE), :] = value[:EDGE, :]
            ypad[z, pl.ds(8 + rows - EDGE, EDGE), :] = value[EDGE:, :]
            ysend[step, 0, pl.ds(z * EDGE, EDGE), :] = value[EDGE:, :]
            ysend[step, 1, pl.ds(z * EDGE, EDGE), :] = value[:EDGE, :]
            if z % per == per - 1:
                for c in y_copies(step, z // per):
                    c.start()
        middle = pl.ds(EDGE, rows - 2 * EDGE)
        for z in range(depth):
            ypad[z, pl.ds(8 + EDGE, rows - 2 * EDGE), :] = pass_x(
                img[z, middle, :], shifts[step, 0, z, middle, :])
        w = cubic_weights(fractions[step, 1])

        def pass_y(part, z):
            for start, count, at in part[0]:
                f = w[0] * ypad[z, pl.ds(5 + start, count + 3), :]
                for n in range(1, 4):
                    f = f + w[n] * ypad[z, pl.ds(5 + start + n, count + 3), :]
                yf[z, pl.ds(0, count + 3), :] = f
                part[1][step, z, pl.ds(at, count), :] = choose(
                    shifts[step, 1, z, pl.ds(start, count), :],
                    [yf[z, pl.ds(o, count), :] for o in range(4)])

        for z in range(depth):
            pass_y(inner, z)
        for c in z_copies(step, inner):
            c.start()
        for z in range(depth):
            if z % per == 0:
                for c in y_copies(step, z // per):
                    c.wait_recv()
            take_edges(step, z)
            pass_y(outer, z)
        for c in z_copies(step, outer):
            c.start()
        w_z = cubic_weights(fractions[step, 2])

        def pass_z(part):
            pieces, mid, received, _ = part
            for c in z_copies(step, part):
                c.wait_recv()
            size = sum(count for _, count, _ in pieces)

            def layer(k):
                if k < HALO:
                    return received[step, 0, k]
                if k < HALO + depth:
                    return mid[step, k - HALO]
                return received[step, 1, k - HALO - depth]

            for k in range(depth + 3):
                zf[k, pl.ds(0, size), :] = (w_z[0] * layer(k) + w_z[1] * layer(k + 1)
                                            + w_z[2] * layer(k + 2) + w_z[3] * layer(k + 3))
            for z in range(depth):
                for start, count, at in pieces:
                    img[z, pl.ds(start, count), :] = choose(
                        shifts[step, 2, z, pl.ds(start, count), :],
                        [zf[z + o, pl.ds(at, count), :] for o in range(4)])

        pass_z(inner)
        pass_z(outer)
        for chunk in range(chunks):
            for c in y_copies(step, chunk):
                c.wait_send()
        for part in (inner, outer):
            for c in z_copies(step, part):
                c.wait_send()
        return carry

    lax.fori_loop(0, steps, advance, 0)

    for z in range(depth):
        put_edges(steps, z, img[z])
    copies = [c for chunk in range(chunks) for c in y_copies(steps, chunk)] + [
        copy(img.at[depth - 1], grecv.at[0], gs_send.at[0], gs_recv.at[0], at_z(1)),
        copy(img.at[0], grecv.at[1], gs_send.at[1], gs_recv.at[1], at_z(-1)),
    ]
    for c in copies:
        c.start()
    fetches[1].wait()
    for z in range(depth):
        u = img[z]
        deformed[z] = u
        forces[pl.ds(z * rows, rows), :] = (
            (u - target[z]) * ((rolled(u, -1, 1) - rolled(u, 1, 1)) * 0.5))
    for c in copies:
        c.wait()
    for z in range(depth):
        take_edges(steps, z)
        mismatch = img[z] - target[z]
        grad = (ypad[z, pl.ds(9, rows), :] - ypad[z, pl.ds(7, rows), :]) * 0.5
        forces[pl.ds((depth + z) * rows, rows), :] = mismatch * grad
        above = img[z + 1] if z + 1 < depth else grecv[1]
        below = img[z - 1] if z > 0 else grecv[0]
        forces[pl.ds((2 * depth + z) * rows, rows), :] = mismatch * ((above - below) * 0.5)

    dc, rc, wc = depth // 2, rows // 2, width // 2
    for c in range(3):
        for z in range(dc):
            base = (c * depth + 2 * z) * rows
            zsum[pl.ds((c * dc + z) * rows, rows), :] = (
                forces[pl.ds(base, rows), :] + forces[pl.ds(base + rows, rows), :])
    fetches[7].wait()
    fetches[9].wait()
    high, low = split(zsum[...])
    f32dot = functools.partial(jnp.dot, preferred_element_type=jnp.float32)
    summed = f32dot(high, pair_x[...]) + f32dot(low, pair_x[...])
    high, low = split(summed)
    coarse[0] = f32dot(pair_y[...], high) + f32dot(pair_y[...], low)
    gathers = [copy(coarse.at[0], coarse.at[d], cs_send.at[d - 1], cs_recv.at[d - 1], at_z(-d))
               for d in range(1, nz)]
    for c in gathers:
        c.start()
    sides = [[copy(coarse.at[d], left.at[d], hs_send.at[0, d], hs_recv.at[0, d], at_y(1)),
              copy(coarse.at[d], right.at[d], hs_send.at[1, d], hs_recv.at[1, d], at_y(-1))]
             for d in range(nz)]
    for c in sides[0]:
        c.start()

    for i in (3, 4, 5):
        fetches[i].wait()
    high, low = split(forces[...])
    ghat[...] = dot3(high, low, hart_hi[...], hart_lo[...])
    for k in range(cz):
        g = ghat[pl.ds(k * rows, rows), :]
        msend[pl.ds(k, 1), :] = jnp.sum(g * tables[0], axis=0, keepdims=True)
        msend[pl.ds(cz + k, 1), :] = jnp.sum(g * tables[1], axis=0, keepdims=True)
    moments = [copy(msend, mrecv.at[d - 1], ms_send.at[d - 1], ms_recv.at[d - 1], at_y(d))
               for d in range(1, ny)]
    for c in moments:
        c.start()
    for d in sorted(range(1, nz), key=lambda d: min(d, nz - d)):
        gathers[d - 1].wait()
        for c in sides[d]:
            c.start()
    for c in moments:
        c.wait()
    fetches[6].wait()
    from_left = hops[pl.ds(ny - 1, 1), :] * msend[pl.ds(0, cz), :]
    from_right = hops[pl.ds(ny - 1, 1), :] * msend[pl.ds(cz, cz), :]
    for m in range(1, ny):
        from_left = from_left + hops[pl.ds(m - 1, 1), :] * mrecv[m - 1, pl.ds(0, cz), :]
        from_right = from_right + hops[pl.ds(m - 1, 1), :] * mrecv[ny - m - 1, pl.ds(cz, cz), :]
    levels = (tables.shape[0] - 5) // 2
    for k in range(cz):
        g = ghat[pl.ds(k * rows, rows), :]
        down, up = g, g
        for level in range(levels):
            down = down + tables[5 + level] * rolled(down, 1 << level, 0)
            up = up + tables[5 + levels + level] * rolled(up, -(1 << level), 0)
        s = (tables[4] * (down + (up - g)) + tables[2] * from_left[k:k + 1, :]
             + tables[3] * from_right[k:k + 1, :])
        high, low = split(s)
        fhi[pl.ds(k * rows, rows), :] = high
        flo[pl.ds(k * rows, rows), :] = low
    ghat[...] = dot3(fhi[...], flo[...], hart_hi[...], hart_lo[...])

    for pair in sides:
        for c in pair:
            c.wait()
    theta, factors = turn_factors(CHEB)
    for d in range(nz):
        for c in range(3):
            for zl in range(dc):
                part = pl.ds((c * dc + zl) * rc, rc)
                for i, source in enumerate((left, coarse, right)):
                    value = source[d, part, :]
                    resid[d * dc + zl, c, pl.ds(i * rc, rc), :] = value
                    dir_a[d * dc + zl, c, pl.ds(i * rc, rc), :] = value * (1.0 / theta)
    total = nz * dc
    for c in range(3):
        for zl in range(dc):
            solved[pl.ds((c * dc + zl) * rc, rc), :] = dir_a[zl, c, pl.ds(rc, rc), :]
    now, later = dir_a, dir_b
    for turn, (keep, add) in enumerate(factors):
        reach = len(factors) - 1 - turn
        count = min(total, dc + 2 * reach)

        def relax(i, carry, now=now, later=later, reach=reach, keep=keep, add=add):
            z = lax.rem(i + (total * CHEB - reach), total)
            above, below = lax.rem(z + 1, total), lax.rem(z + (total - 1), total)
            for c in range(3):
                v = now[z, c]
                beside = now[above, c] + now[below, c]
                beside = beside + rolled(v, -1, 0) + rolled(v, 1, 0)
                beside = beside + rolled(v, -1, 1) + rolled(v, 1, 1)
                res = resid[z, c] - ((SHIFT + 6.0) * v - beside)
                resid[z, c] = res
                later[z, c] = keep * v + add * res
            return carry

        lax.fori_loop(0, count, relax, 0)
        for c in range(3):
            for zl in range(dc):
                part = pl.ds((c * dc + zl) * rc, rc)
                solved[part, :] = solved[part, :] + later[zl, c, pl.ds(rc, rc), :]
        now, later = later, now

    fetches[8].wait()
    fetches[10].wait()
    high, low = split(solved[...])
    tall = f32dot(spread_y[...], high) + f32dot(spread_y[...], low)
    high, low = split(tall)
    zsum[...] = f32dot(high, spread_x[...]) + f32dot(low, spread_x[...])
    for c in range(3):
        for z in range(depth):
            fine = zsum[pl.ds((c * dc + z // 2) * rows, rows), :]
            update[c, z] = -(ghat[pl.ds((c * depth + z) * rows, rows), :] + fine)


def on_device(template, target, shifts, fractions, *, ny, nz):
    depth, rows, width = template.shape
    steps = shifts.shape[0]
    dc, rc, wc = depth // 2, rows // 2, width // 2
    cz = 3 * depth
    hart_hi, hart_lo, tables, hops = make_tables(rows, width, ny)
    pair_x = np.kron(np.eye(wc), np.full((2, 1), 0.125)).astype(jnp.bfloat16)
    spread_x = np.kron(np.eye(wc), np.ones((1, 2))).astype(jnp.bfloat16)
    pair_y = np.kron(np.eye(3 * dc * rc), np.ones((1, 2))).astype(jnp.bfloat16)
    spread_y = np.ascontiguousarray(pair_y.T)
    f32, bf16 = jnp.float32, jnp.bfloat16
    vmem, dma = pltpu.VMEM, pltpu.SemaphoreType.DMA
    total = nz * dc
    scratch = [
        vmem((depth, rows, width), f32),
        vmem((depth, rows + 16, width), f32),
        vmem((depth, rows + 8, width), f32),
        vmem((steps + 1, 2, depth * EDGE, width), f32),
        vmem((steps + 1, 2, depth * EDGE, width), f32),
        vmem((steps, depth, rows - 2 * EDGE, width), f32),
        vmem((steps, 2, HALO, rows - 2 * EDGE, width), f32),
        vmem((steps, depth, 2 * EDGE, width), f32),
        vmem((steps, 2, HALO, 2 * EDGE, width), f32),
        vmem((depth + 3, rows, width), f32),
        vmem((2, rows, width), f32),
        vmem((cz * rows, width), f32),
        vmem((cz * rows, width), f32),
        vmem((2 * cz, width), f32),
        vmem((ny - 1, 2 * cz, width), f32),
        vmem((nz, 3 * dc * rc, wc), f32),
        vmem((nz, 3 * dc * rc, wc), f32),
        vmem((nz, 3 * dc * rc, wc), f32),
        vmem((total, 3, 3 * rc, wc), f32),
        vmem((total, 3, 3 * rc, wc), f32),
        vmem((total, 3, 3 * rc, wc), f32),
        vmem((3 * dc * rc, wc), f32),
        vmem((3 * dc * rows, width), f32),
        vmem((cz * rows, width), bf16),
        vmem((cz * rows, width), bf16),
        dma((steps + 1, 2, depth * EDGE // 8)), dma((steps + 1, 2, depth * EDGE // 8)),
        dma((steps, 2, 2)), dma((steps, 2, 2)),
        dma((2,)), dma((2,)),
        dma((ny - 1,)), dma((ny - 1,)),
        dma((nz - 1,)), dma((nz - 1,)),
        dma((2, nz)), dma((2, nz)),
    ]
    spec = pl.BlockSpec(memory_space=pltpu.VMEM)
    smem = pl.BlockSpec(memory_space=pltpu.SMEM)
    hbm = pl.BlockSpec(memory_space=pltpu.HBM)
    operands = [template, target, shifts, jnp.asarray(hart_hi), jnp.asarray(hart_lo),
                jnp.asarray(tables), jnp.asarray(hops), jnp.asarray(pair_x),
                jnp.asarray(spread_x), jnp.asarray(pair_y), jnp.asarray(spread_y)]
    held = [vmem(x.shape, x.dtype) for x in operands]
    scratch = held + [dma((len(operands),)), dma((steps,))] + scratch
    return tuple(pl.pallas_call(
        functools.partial(kernel, ny, nz),
        out_shape=(vmem((3, depth, rows, width), f32), vmem((depth, rows, width), f32)),
        in_specs=[smem] + [hbm] * len(operands),
        out_specs=(spec, spec),
        scratch_shapes=scratch,
        compiler_params=pltpu.CompilerParams(
            collective_id=0, has_side_effects=True),
    )(fractions, *operands))


def solution(mesh):
    return jax.shard_map(
        functools.partial(on_device, ny=mesh.shape["gy"], nz=mesh.shape["gz"]),
        mesh=mesh,
        in_specs=(P("gz", "gy", None), P("gz", "gy", None), P(None, None, "gz", "gy", None), P()),
        out_specs=(P(None, "gz", "gy", None), P("gz", "gy", None)),
        check_vma=False,
    )
```

```python
import functools

import jax
import jax.numpy as jnp
import numpy as np
from jax import lax
from jax.experimental import pallas as pl
from jax.experimental.pallas import tpu as pltpu
from jax.sharding import PartitionSpec as P

CHEB = 8
DAMPING = 0.25
ACROSS_WEIGHT = 0.0625
ALONG_SCALE = 32.0
SHIFT = 0.25
MESH = pl.DeviceIdType.MESH
EDGE = 4
HALO = 3


def cubic_weights(fraction):
    return (
        -fraction * (fraction - 1.0) * (fraction - 2.0) / 6.0,
        (fraction + 1.0) * (fraction - 1.0) * (fraction - 2.0) / 2.0,
        -(fraction + 1.0) * fraction * (fraction - 2.0) / 2.0,
        (fraction + 1.0) * fraction * (fraction - 1.0) / 6.0,
    )


def turn_factors(count):
    low, high = SHIFT, SHIFT + 12.0
    theta, delta = (high + low) / 2.0, (high - low) / 2.0
    sigma = theta / delta
    now = 1.0 / sigma
    factors = []
    for _ in range(count - 1):
        after = 1.0 / (2.0 * sigma - now)
        factors.append((after * now, 2.0 * after / delta))
        now = after
    return theta, factors


def make_tables(rows, length_x, peers):
    length_y = rows * peers
    index = np.arange(length_x)
    angle = 2.0 * np.pi / length_x * (np.outer(index, index) % length_x)
    hartley = np.cos(angle) + np.sin(angle)
    weight = (length_y / ALONG_SCALE) ** 2
    a = DAMPING + 4.0 * ACROSS_WEIGHT * np.sin(np.pi * index / length_x) ** 2
    half = a / (2.0 * weight)
    r = 1.0 / (1.0 + half + np.sqrt(half * (half + 2.0)))
    y = np.arange(rows)[:, None]
    scale = 1.0 / (weight * (1.0 / r - r) * length_x)
    down, up, stride = [], [], 1
    while stride < rows:
        down.append(np.where(y >= stride, r ** stride, 0.0))
        up.append(np.where(y < rows - stride, r ** stride, 0.0))
        stride *= 2
    tables = [r ** (rows - 1 - y), r ** y, scale * r ** (y + 1), scale * r ** (rows - y),
              scale + 0.0 * r * y] + down + up
    m = np.arange(peers)[:, None]
    hops = r ** (rows * m) / (1.0 - r ** length_y)
    high = hartley.astype(jnp.bfloat16)
    low = (hartley - high.astype(np.float64)).astype(jnp.bfloat16)
    return high, low, np.stack(tables).astype(np.float32), hops.astype(np.float32)


def cas(length):
    index = np.arange(length)
    angle = 2.0 * np.pi / length * (np.outer(index, index) % length)
    return np.cos(angle) + np.sin(angle)


def in_two(table):
    high = table.astype(jnp.bfloat16)
    return high, (table - high.astype(np.float64)).astype(jnp.bfloat16)


def far_layers(total):
    return min(total // 2, CHEB - 1) + 1


def make_coarse(width, total, length_y):
    half = width // 2
    pair = np.kron(np.eye(half), np.full((2, 1), 0.125))
    fold = in_two(pair @ cas(half))
    spread = in_two(cas(half) @ np.kron(np.eye(half), np.ones((1, 2))) / half)
    x, y, z = [2.0 * np.cos(2.0 * np.pi * np.arange(n) / n) for n in (half, length_y, total)]
    symbol = SHIFT + 6.0 - (z[:, None, None] + y[None, :, None] + x[None, None, :])
    theta, factors = turn_factors(CHEB)
    residual = np.ones_like(symbol)
    direction = residual / theta
    gain = direction
    for keep, add in factors:
        residual = residual - symbol * direction
        direction = keep * direction + add * residual
        gain = gain + direction
    taps = []
    for dz in range(far_layers(total)):
        in_z = np.cos(2.0 * np.pi * dz * np.arange(total) / total) / total
        plane = np.tensordot(in_z, gain, 1)
        for dy in range(CHEB - dz):
            in_y = np.cos(2.0 * np.pi * dy * np.arange(length_y) / length_y) / length_y
            taps.append(in_y @ plane)
    return fold + spread + (np.stack(taps).astype(np.float32),)


def dot3(high, low, table_high, table_low):
    f = functools.partial(jnp.dot, preferred_element_type=jnp.float32)
    return f(high, table_high) + (f(low, table_high) + f(high, table_low))


def split(value):
    high = value.astype(jnp.bfloat16)
    return high, (value - high.astype(jnp.float32)).astype(jnp.bfloat16)


def choose(shift, options):
    minus2, minus1, zero, one = options
    result = jnp.where(shift == 0, zero, one)
    result = jnp.where(shift == -1, minus1, result)
    return jnp.where(shift == -2, minus2, result)


def kernel(ny, nz, fractions, *refs):
    count = 14
    sources, (update, deformed), rest = refs[:count], refs[count:count + 2], refs[count + 2:]
    held, fetch_sems, shift_sems = rest[:count], rest[count], rest[count + 1]
    step_count = held[2].shape[0]
    fetches = {}
    for i in (0, 1, *range(3, count)):
        fetches[i] = pltpu.make_async_copy(sources[i], held[i], fetch_sems.at[i])

    def fetch_shifts(step):
        return pltpu.make_async_copy(sources[2].at[step], held[2].at[step], shift_sems.at[step])

    fetches[0].start()
    for step in range(step_count):
        fetch_shifts(step).start()
    for i in (1, 7, 8, 11, 3, 4, 5, 6, 13, 9, 10, 12):
        fetches[i].start()
    body(ny, nz, fractions, fetches, fetch_shifts, *held, update, deformed, *rest[count + 2:])


def body(ny, nz, fractions, fetches, fetch_shifts, template, target, shifts, hart_hi, hart_lo,
         tables, hops, fold_hi, fold_lo, spread_hi, spread_lo, pair_y, spread_y, taps,
         update, deformed, img, ypad, yf, ysend, yrecv, zmid, zrecv, zmid_edge, zrecv_edge,
           zf, grecv, forces, ghat, msend, mrecv, coarse, parts, arrived, mixed,
           zsum, fhi, flo, ys_send, ys_recv, zs_send, zs_recv, gs_send, gs_recv, ms_send, ms_recv,
           cs_send, cs_recv, hs_send, hs_recv):
    depth, rows, width = template.shape
    steps = shifts.shape[0]
    cz = 3 * depth
    me_y, me_z = lax.axis_index("gy"), lax.axis_index("gz")

    def at_y(offset):
        return (lax.rem(me_y + (offset + ny), ny), me_z)

    def at_z(offset):
        return (me_y, lax.rem(me_z + (offset + nz), nz))

    def copy(src, dst, send, recv, device):
        return pltpu.make_async_remote_copy(
            src_ref=src, dst_ref=dst, send_sem=send, recv_sem=recv, device_id=device,
            device_id_type=MESH)

    barrier = pltpu.get_barrier_semaphore()
    for d in range(1, ny):
        pl.semaphore_signal(barrier, inc=1, device_id=at_y(d), device_id_type=MESH)
    for d in range(1, nz):
        pl.semaphore_signal(barrier, inc=1, device_id=at_z(d), device_id_type=MESH)

    def rolled(value, by, axis):
        return pltpu.roll(value, by % value.shape[axis], axis)

    mixed[...] = jnp.zeros_like(mixed)
    fetches[0].wait()
    for z in range(depth):
        img[z] = template[z]
    pl.semaphore_wait(barrier, ny + nz - 2)

    chunks = depth * EDGE // 8
    per = depth // chunks

    def y_copies(step, chunk):
        part = pl.ds(chunk * 8, 8)
        return [copy(ysend.at[step, side, part], yrecv.at[step, side, part],
                     ys_send.at[step, side, chunk], ys_recv.at[step, side, chunk],
                     at_y(1 - 2 * side)) for side in range(2)]

    inner = (((EDGE, rows - 2 * EDGE, 0),), zmid, zrecv, 0)
    outer = (((0, EDGE, 0), (rows - EDGE, EDGE, EDGE)), zmid_edge, zrecv_edge, 1)

    def z_copies(step, part):
        _, mid, received, which = part
        return [copy(mid.at[step, pl.ds(0 if side else depth - HALO, HALO)],
                     received.at[step, side], zs_send.at[step, side, which],
                     zs_recv.at[step, side, which], at_z(1 - 2 * side)) for side in range(2)]

    def put_edges(step, z, value):
        ypad[z, pl.ds(8, rows), :] = value
        ysend[step, 0, pl.ds(z * EDGE, EDGE), :] = value[rows - EDGE:, :]
        ysend[step, 1, pl.ds(z * EDGE, EDGE), :] = value[:EDGE, :]

    def take_edges(step, z):
        ypad[z, pl.ds(8 - EDGE, EDGE), :] = yrecv[step, 0, pl.ds(z * EDGE, EDGE), :]
        ypad[z, pl.ds(8 + rows, EDGE), :] = yrecv[step, 1, pl.ds(z * EDGE, EDGE), :]

    def advance(step, carry):
        fetch_shifts(step).wait()
        w = cubic_weights(fractions[step, 0])

        def pass_x(u, shift):
            f = (w[0] * rolled(u, 1, 1) + w[1] * u + w[2] * rolled(u, -1, 1)
                 + w[3] * rolled(u, -2, 1))
            return choose(shift, (rolled(f, 2, 1), rolled(f, 1, 1), f, rolled(f, -1, 1)))

        first, last = pl.ds(0, EDGE), pl.ds(rows - EDGE, EDGE)
        for z in range(depth):
            value = pass_x(
                jnp.concatenate([img[z, first, :], img[z, last, :]], axis=0),
                jnp.concatenate([shifts[step, 0, z, first, :], shifts[step, 0, z, last, :]],
                                axis=0))
            ypad[z, pl.ds(8, EDGE), :] = value[:EDGE, :]
            ypad[z, pl.ds(8 + rows - EDGE, EDGE), :] = value[EDGE:, :]
            ysend[step, 0, pl.ds(z * EDGE, EDGE), :] = value[EDGE:, :]
            ysend[step, 1, pl.ds(z * EDGE, EDGE), :] = value[:EDGE, :]
            if z % per == per - 1:
                for c in y_copies(step, z // per):
                    c.start()
        middle = pl.ds(EDGE, rows - 2 * EDGE)
        for z in range(depth):
            ypad[z, pl.ds(8 + EDGE, rows - 2 * EDGE), :] = pass_x(
                img[z, middle, :], shifts[step, 0, z, middle, :])
        w = cubic_weights(fractions[step, 1])

        def pass_y(part, z):
            for start, count, at in part[0]:
                f = w[0] * ypad[z, pl.ds(5 + start, count + 3), :]
                for n in range(1, 4):
                    f = f + w[n] * ypad[z, pl.ds(5 + start + n, count + 3), :]
                yf[z, pl.ds(0, count + 3), :] = f
                part[1][step, z, pl.ds(at, count), :] = choose(
                    shifts[step, 1, z, pl.ds(start, count), :],
                    [yf[z, pl.ds(o, count), :] for o in range(4)])

        for z in range(depth):
            pass_y(inner, z)
        for c in z_copies(step, inner):
            c.start()
        for z in range(depth):
            if z % per == 0:
                for c in y_copies(step, z // per):
                    c.wait_recv()
            take_edges(step, z)
            pass_y(outer, z)
        for c in z_copies(step, outer):
            c.start()
        w_z = cubic_weights(fractions[step, 2])

        def pass_z(part):
            pieces, mid, received, _ = part
            for c in z_copies(step, part):
                c.wait_recv()
            size = sum(count for _, count, _ in pieces)

            def layer(k):
                if k < HALO:
                    return received[step, 0, k]
                if k < HALO + depth:
                    return mid[step, k - HALO]
                return received[step, 1, k - HALO - depth]

            for k in range(depth + 3):
                zf[k, pl.ds(0, size), :] = (w_z[0] * layer(k) + w_z[1] * layer(k + 1)
                                            + w_z[2] * layer(k + 2) + w_z[3] * layer(k + 3))
            for z in range(depth):
                for start, count, at in pieces:
                    img[z, pl.ds(start, count), :] = choose(
                        shifts[step, 2, z, pl.ds(start, count), :],
                        [zf[z + o, pl.ds(at, count), :] for o in range(4)])

        pass_z(inner)
        pass_z(outer)
        for chunk in range(chunks):
            for c in y_copies(step, chunk):
                c.wait_send()
        for part in (inner, outer):
            for c in z_copies(step, part):
                c.wait_send()
        return carry

    lax.fori_loop(0, steps, advance, 0)

    for z in range(depth):
        put_edges(steps, z, img[z])
    copies = [c for chunk in range(chunks) for c in y_copies(steps, chunk)] + [
        copy(img.at[depth - 1], grecv.at[0], gs_send.at[0], gs_recv.at[0], at_z(1)),
        copy(img.at[0], grecv.at[1], gs_send.at[1], gs_recv.at[1], at_z(-1)),
    ]
    for c in copies:
        c.start()
    fetches[1].wait()
    for z in range(depth):
        u = img[z]
        deformed[z] = u
        forces[pl.ds(z * rows, rows), :] = (
            (u - target[z]) * ((rolled(u, -1, 1) - rolled(u, 1, 1)) * 0.5))
    for c in copies:
        c.wait()
    for z in range(depth):
        take_edges(steps, z)
        mismatch = img[z] - target[z]
        grad = (ypad[z, pl.ds(9, rows), :] - ypad[z, pl.ds(7, rows), :]) * 0.5
        forces[pl.ds((depth + z) * rows, rows), :] = mismatch * grad
        above = img[z + 1] if z + 1 < depth else grecv[1]
        below = img[z - 1] if z > 0 else grecv[0]
        forces[pl.ds((2 * depth + z) * rows, rows), :] = mismatch * ((above - below) * 0.5)

    dc, rc, wc = depth // 2, rows // 2, width // 2
    for c in range(3):
        for z in range(dc):
            base = (c * depth + 2 * z) * rows
            zsum[pl.ds((c * dc + z) * rows, rows), :] = (
                forces[pl.ds(base, rows), :] + forces[pl.ds(base + rows, rows), :])
    for i in (7, 8, 11):
        fetches[i].wait()
    f32dot = functools.partial(jnp.dot, preferred_element_type=jnp.float32)
    high, low = split(zsum[...])
    high, low = split(dot3(high, low, fold_hi[...], fold_lo[...]))
    coarse[0] = f32dot(pair_y[...], high) + f32dot(pair_y[...], low)
    gathers = []
    for k in range(nz - 1):
        away = jnp.where(me_z < nz // 2, nz - 1 - k, k)
        away = away + jnp.where(me_z < nz // 2, -(away <= me_z).astype(jnp.int32),
                                (away >= me_z).astype(jnp.int32))
        slot = lax.rem(me_z - away + nz, nz)
        gathers.append(copy(coarse.at[0], coarse.at[slot], cs_send.at[slot - 1],
                            cs_recv.at[slot - 1], (me_y, away)))
    for c in gathers:
        c.start()

    for i in (3, 4, 5):
        fetches[i].wait()
    high, low = split(forces[...])
    ghat[...] = dot3(high, low, hart_hi[...], hart_lo[...])
    for k in range(cz):
        g = ghat[pl.ds(k * rows, rows), :]
        msend[pl.ds(k, 1), :] = jnp.sum(g * tables[0], axis=0, keepdims=True)
        msend[pl.ds(cz + k, 1), :] = jnp.sum(g * tables[1], axis=0, keepdims=True)
    moments = [copy(msend, mrecv.at[d - 1], ms_send.at[d - 1], ms_recv.at[d - 1], at_y(d))
               for d in range(1, ny)]
    for c in moments:
        c.start()
    fetches[13].wait()
    for d in range(1, nz):
        copy(coarse.at[0], coarse.at[d], cs_send.at[d - 1], cs_recv.at[d - 1], at_z(-d)).wait()
    total, far = nz * dc, far_layers(nz * dc)
    lanes = min(wc, 128)
    for c in range(3):
        for h in range(wc // lanes):
            across = pl.ds(h * lanes, lanes)

            def level(z, c=c, across=across):
                return coarse[z % total // dc, pl.ds((c * dc + z % dc) * rc, rc), across]

            for a in range(dc):
                for dz in range(far):
                    value = level(a + dz)
                    if 0 < dz and 2 * dz != total:
                        value = value + level(a + total - dz)
                    mixed[h, a * far + dz, pl.ds(rc, rc), :] = value
            for a in range(dc):
                sums = [None] * 3

                def add(side, value):
                    sums[side] = value if sums[side] is None else sums[side] + value

                row = 0
                for dz in range(far):
                    for dy in range(CHEB - dz):
                        tap = taps[pl.ds(row, 1), across]
                        row += 1
                        at = [mixed[h, a * far + dz, pl.ds(o, rc), :]
                              for o in (dy, rc - dy, rc + dy, 2 * rc - dy)]
                        if dy == 0:
                            add(0, tap * at[1])
                        else:
                            add(0, tap * (at[1] + at[2]))
                            add(1, tap * at[0])
                            add(2, tap * at[3])
                for side in range(3):
                    parts[side, pl.ds((c * dc + a) * rc, rc), across] = sums[side]
    sides = [copy(parts.at[1], arrived.at[0], hs_send.at[0], hs_recv.at[0], at_y(-1)),
             copy(parts.at[2], arrived.at[1], hs_send.at[1], hs_recv.at[1], at_y(1))]
    for c in sides:
        c.start()
    for c in moments:
        c.wait()
    fetches[6].wait()
    from_left = hops[pl.ds(ny - 1, 1), :] * msend[pl.ds(0, cz), :]
    from_right = hops[pl.ds(ny - 1, 1), :] * msend[pl.ds(cz, cz), :]
    for m in range(1, ny):
        from_left = from_left + hops[pl.ds(m - 1, 1), :] * mrecv[m - 1, pl.ds(0, cz), :]
        from_right = from_right + hops[pl.ds(m - 1, 1), :] * mrecv[ny - m - 1, pl.ds(cz, cz), :]
    levels = (tables.shape[0] - 5) // 2
    for k in range(cz):
        g = ghat[pl.ds(k * rows, rows), :]
        down, up = g, g
        for level in range(levels):
            down = down + tables[5 + level] * rolled(down, 1 << level, 0)
            up = up + tables[5 + levels + level] * rolled(up, -(1 << level), 0)
        s = (tables[4] * (down + (up - g)) + tables[2] * from_left[k:k + 1, :]
             + tables[3] * from_right[k:k + 1, :])
        high, low = split(s)
        fhi[pl.ds(k * rows, rows), :] = high
        flo[pl.ds(k * rows, rows), :] = low
    ghat[...] = dot3(fhi[...], flo[...], hart_hi[...], hart_lo[...])

    for i in (9, 10, 12):
        fetches[i].wait()
    for c in sides:
        c.wait()
    high, low = split(parts[0] + (arrived[0] + arrived[1]))
    tall = f32dot(spread_y[...], high) + f32dot(spread_y[...], low)
    high, low = split(tall)
    zsum[...] = dot3(high, low, spread_hi[...], spread_lo[...])
    for c in range(3):
        for z in range(depth):
            fine = zsum[pl.ds((c * dc + z // 2) * rows, rows), :]
            update[c, z] = -(ghat[pl.ds((c * depth + z) * rows, rows), :] + fine)


def on_device(template, target, shifts, fractions, *, ny, nz):
    depth, rows, width = template.shape
    steps = shifts.shape[0]
    dc, rc, wc = depth // 2, rows // 2, width // 2
    cz = 3 * depth
    hart_hi, hart_lo, tables, hops = make_tables(rows, width, ny)
    fold_hi, fold_lo, spread_hi, spread_lo, taps = make_coarse(width, nz * dc, ny * rc)
    pair_y = np.kron(np.eye(3 * dc * rc), np.ones((1, 2))).astype(jnp.bfloat16)
    spread_y = np.ascontiguousarray(pair_y.T)
    f32, bf16 = jnp.float32, jnp.bfloat16
    vmem, dma = pltpu.VMEM, pltpu.SemaphoreType.DMA
    scratch = [
        vmem((depth, rows, width), f32),
        vmem((depth, rows + 16, width), f32),
        vmem((depth, rows + 8, width), f32),
        vmem((steps + 1, 2, depth * EDGE, width), f32),
        vmem((steps + 1, 2, depth * EDGE, width), f32),
        vmem((steps, depth, rows - 2 * EDGE, width), f32),
        vmem((steps, 2, HALO, rows - 2 * EDGE, width), f32),
        vmem((steps, depth, 2 * EDGE, width), f32),
        vmem((steps, 2, HALO, 2 * EDGE, width), f32),
        vmem((depth + 3, rows, width), f32),
        vmem((2, rows, width), f32),
        vmem((cz * rows, width), f32),
        vmem((cz * rows, width), f32),
        vmem((2 * cz, width), f32),
        vmem((ny - 1, 2 * cz, width), f32),
        vmem((nz, 3 * dc * rc, wc), f32),
        vmem((3, 3 * dc * rc, wc), f32),
        vmem((2, 3 * dc * rc, wc), f32),
        vmem((-(-wc // 128), dc * far_layers(nz * dc), 3 * rc, min(wc, 128)), f32),
        vmem((3 * dc * rows, width), f32),
        vmem((cz * rows, width), bf16),
        vmem((cz * rows, width), bf16),
        dma((steps + 1, 2, depth * EDGE // 8)), dma((steps + 1, 2, depth * EDGE // 8)),
        dma((steps, 2, 2)), dma((steps, 2, 2)),
        dma((2,)), dma((2,)),
        dma((ny - 1,)), dma((ny - 1,)),
        dma((nz - 1,)), dma((nz - 1,)),
        dma((2,)), dma((2,)),
    ]
    spec = pl.BlockSpec(memory_space=pltpu.VMEM)
    smem = pl.BlockSpec(memory_space=pltpu.SMEM)
    hbm = pl.BlockSpec(memory_space=pltpu.HBM)
    operands = [template, target, shifts, jnp.asarray(hart_hi), jnp.asarray(hart_lo),
                *map(jnp.asarray, (tables, hops, fold_hi, fold_lo, spread_hi, spread_lo, pair_y,
                                   spread_y, taps))]
    held = [vmem(x.shape, x.dtype) for x in operands]
    scratch = held + [dma((len(operands),)), dma((steps,))] + scratch
    return tuple(pl.pallas_call(
        functools.partial(kernel, ny, nz),
        out_shape=(vmem((3, depth, rows, width), f32), vmem((depth, rows, width), f32)),
        in_specs=[smem] + [hbm] * len(operands),
        out_specs=(spec, spec),
        scratch_shapes=scratch,
        compiler_params=pltpu.CompilerParams(
            collective_id=0, has_side_effects=True),
    )(fractions, *operands))


def solution(mesh):
    return jax.shard_map(
        functools.partial(on_device, ny=mesh.shape["gy"], nz=mesh.shape["gz"]),
        mesh=mesh,
        in_specs=(P("gz", "gy", None), P("gz", "gy", None), P(None, None, "gz", "gy", None), P()),
        out_specs=(P(None, "gz", "gy", None), P("gz", "gy", None)),
        check_vma=False,
    )
```

```python
import functools

import jax
import jax.numpy as jnp
import numpy as np
from jax import lax
from jax.experimental import pallas as pl
from jax.experimental.pallas import tpu as pltpu
from jax.sharding import PartitionSpec as P

CHEB = 8
DAMPING = 0.25
ACROSS_WEIGHT = 0.0625
ALONG_SCALE = 32.0
SHIFT = 0.25
MESH = pl.DeviceIdType.MESH
EDGE = 4
HALO = 3


def cubic_weights(fraction):
    return (
        -fraction * (fraction - 1.0) * (fraction - 2.0) / 6.0,
        (fraction + 1.0) * (fraction - 1.0) * (fraction - 2.0) / 2.0,
        -(fraction + 1.0) * fraction * (fraction - 2.0) / 2.0,
        (fraction + 1.0) * fraction * (fraction - 1.0) / 6.0,
    )


def turn_factors(count):
    low, high = SHIFT, SHIFT + 12.0
    theta, delta = (high + low) / 2.0, (high - low) / 2.0
    sigma = theta / delta
    now = 1.0 / sigma
    factors = []
    for _ in range(count - 1):
        after = 1.0 / (2.0 * sigma - now)
        factors.append((after * now, 2.0 * after / delta))
        now = after
    return theta, factors


def make_tables(rows, length_x, peers):
    length_y = rows * peers
    index = np.arange(length_x)
    angle = 2.0 * np.pi / length_x * (np.outer(index, index) % length_x)
    hartley = np.cos(angle) + np.sin(angle)
    weight = (length_y / ALONG_SCALE) ** 2
    a = DAMPING + 4.0 * ACROSS_WEIGHT * np.sin(np.pi * index / length_x) ** 2
    half = a / (2.0 * weight)
    r = 1.0 / (1.0 + half + np.sqrt(half * (half + 2.0)))
    y = np.arange(rows)[:, None]
    scale = 1.0 / (weight * (1.0 / r - r) * length_x)
    down, up, stride = [], [], 1
    while stride < rows:
        down.append(np.where(y >= stride, r ** stride, 0.0))
        up.append(np.where(y < rows - stride, r ** stride, 0.0))
        stride *= 2
    tables = [r ** (rows - 1 - y), r ** y, scale * r ** (y + 1), scale * r ** (rows - y),
              scale + 0.0 * r * y] + down + up
    m = np.arange(peers)[:, None]
    hops = r ** (rows * m) / (1.0 - r ** length_y)
    high = hartley.astype(jnp.bfloat16)
    low = (hartley - high.astype(np.float64)).astype(jnp.bfloat16)
    return high, low, np.stack(tables).astype(np.float32), hops.astype(np.float32)


def cas(length):
    index = np.arange(length)
    angle = 2.0 * np.pi / length * (np.outer(index, index) % length)
    return np.cos(angle) + np.sin(angle)


def in_two(table):
    high = table.astype(jnp.bfloat16)
    return high, (table - high.astype(np.float64)).astype(jnp.bfloat16)


def far_layers(total):
    return min(total // 2, CHEB - 1) + 1


def make_coarse(width, total, length_y):
    half = width // 2
    pair = np.kron(np.eye(half), np.full((2, 1), 0.125))
    fold = in_two(pair @ cas(half))
    spread = in_two(cas(half) @ np.kron(np.eye(half), np.ones((1, 2))) / half)
    x, y, z = [2.0 * np.cos(2.0 * np.pi * np.arange(n) / n) for n in (half, length_y, total)]
    symbol = SHIFT + 6.0 - (z[:, None, None] + y[None, :, None] + x[None, None, :])
    theta, factors = turn_factors(CHEB)
    residual = np.ones_like(symbol)
    direction = residual / theta
    gain = direction
    for keep, add in factors:
        residual = residual - symbol * direction
        direction = keep * direction + add * residual
        gain = gain + direction
    taps = []
    for dz in range(far_layers(total)):
        in_z = np.cos(2.0 * np.pi * dz * np.arange(total) / total) / total
        plane = np.tensordot(in_z, gain, 1)
        for dy in range(CHEB - dz):
            in_y = np.cos(2.0 * np.pi * dy * np.arange(length_y) / length_y) / length_y
            taps.append(in_y @ plane)
    return fold + spread + (np.stack(taps).astype(np.float32),)


def dot3(high, low, table_high, table_low):
    f = functools.partial(jnp.dot, preferred_element_type=jnp.float32)
    return f(high, table_high) + (f(low, table_high) + f(high, table_low))


def split(value):
    high = value.astype(jnp.bfloat16)
    return high, (value - high.astype(jnp.float32)).astype(jnp.bfloat16)


def choose(shift, options):
    minus2, minus1, zero, one = options
    result = jnp.where(shift == 0, zero, one)
    result = jnp.where(shift == -1, minus1, result)
    return jnp.where(shift == -2, minus2, result)


def kernel(ny, nz, fractions, *refs):
    count = 14
    sources, (update, deformed), rest = refs[:count], refs[count:count + 2], refs[count + 2:]
    held, fetch_sems, shift_sems = rest[:count], rest[count], rest[count + 1]
    step_count = held[2].shape[0]
    fetches = {}
    for i in (0, 1, *range(3, count)):
        fetches[i] = pltpu.make_async_copy(sources[i], held[i], fetch_sems.at[i])

    def fetch_shifts(step):
        return pltpu.make_async_copy(sources[2].at[step], held[2].at[step], shift_sems.at[step])

    fetches[0].start()
    for step in range(step_count):
        fetch_shifts(step).start()
    for i in (1, 7, 8, 11, 3, 4, 5, 6, 13, 9, 10, 12):
        fetches[i].start()
    body(ny, nz, fractions, fetches, fetch_shifts, sources[2], *held, update, deformed, *rest[count + 2:])


def body(ny, nz, fractions, fetches, fetch_shifts, all_shifts, template, target, shifts, hart_hi, hart_lo,
         tables, hops, fold_hi, fold_lo, spread_hi, spread_lo, pair_y, spread_y, taps,
         update, deformed, img, ypad, yf, ysend, yrecv, zmid, zrecv, zmid_edge, zrecv_edge,
           zf, beyond, zshift, yshift_send, yshift, rim, rim_rows, rim_f, forces, ghat, msend, mrecv, coarse, parts, arrived, mixed,
           zsum, fhi, flo, ys_send, ys_recv, zs_send, zs_recv, rs_send, rs_recv, zh_send, zh_recv, yh_send, yh_recv, ms_send, ms_recv,
           cs_send, cs_recv, hs_send, hs_recv):
    depth, rows, width = template.shape
    steps = shifts.shape[0]
    cz = 3 * depth
    me_y, me_z = lax.axis_index("gy"), lax.axis_index("gz")

    def at_y(offset):
        return (lax.rem(me_y + (offset + ny), ny), me_z)

    def at_z(offset):
        return (me_y, lax.rem(me_z + (offset + nz), nz))

    def copy(src, dst, send, recv, device):
        return pltpu.make_async_remote_copy(
            src_ref=src, dst_ref=dst, send_sem=send, recv_sem=recv, device_id=device,
            device_id_type=MESH)

    barrier = pltpu.get_barrier_semaphore()
    for d in range(1, ny):
        pl.semaphore_signal(barrier, inc=1, device_id=at_y(d), device_id_type=MESH)
    for d in range(1, nz):
        pl.semaphore_signal(barrier, inc=1, device_id=at_z(d), device_id_type=MESH)

    def rolled(value, by, axis):
        return pltpu.roll(value, by % value.shape[axis], axis)

    chunks = depth * EDGE // 8
    per = depth // chunks

    def y_copies(step, chunk):
        part = pl.ds(chunk * 8, 8)
        return [copy(ysend.at[step, side, part], yrecv.at[step, side, part],
                     ys_send.at[step, side, chunk], ys_recv.at[step, side, chunk],
                     at_y(1 - 2 * side)) for side in range(2)]

    inner = (((EDGE, rows - 2 * EDGE, 0),), zmid, zrecv, 0)
    outer = (((0, EDGE, 0), (rows - EDGE, EDGE, EDGE)), zmid_edge, zrecv_edge, 1)

    def z_copies(step, part, halo=HALO, side=None):
        _, mid, received, which = part
        if side is None:
            return [z_copies(step, part, halo, side) for side in range(2)]
        return copy(mid.at[step, pl.ds((1 - side) * (depth - halo), halo)],
                    received.at[step, side, pl.ds(0, halo)], zs_send.at[step, side, which],
                    zs_recv.at[step, side, which], at_z(1 - 2 * side))

    far_side = jnp.where(me_z < nz // 2, 1, 0)

    def start_z(step, part, halo=HALO):
        for side in (far_side, 1 - far_side):
            z_copies(step, part, halo, side).start()

    mine = pl.ds(2 * depth, 2 * depth)

    def rim_copies():
        return [copy(rim.at[mine], rim.at[pl.ds(side * 4 * depth, 2 * depth)],
                     rs_send.at[side], rs_recv.at[side], at_z(1 - 2 * side)) for side in range(2)]

    ahead = [copy(all_shifts.at[steps - 1, 2, depth - 1], zshift.at[0], zh_send.at[0],
                  zh_recv.at[0], at_z(1)),
             copy(all_shifts.at[steps - 1, 2, 0], zshift.at[1], zh_send.at[1], zh_recv.at[1],
                  at_z(-1)),
             copy(yshift_send.at[0], yshift.at[0], yh_send.at[0], yh_recv.at[0], at_y(1)),
             copy(yshift_send.at[1], yshift.at[1], yh_send.at[1], yh_recv.at[1], at_y(-1))]

    def take_edges(step, z):
        ypad[z, pl.ds(8 - EDGE, EDGE), :] = yrecv[step, 0, pl.ds(z * EDGE, EDGE), :]
        ypad[z, pl.ds(8 + rows, EDGE), :] = yrecv[step, 1, pl.ds(z * EDGE, EDGE), :]

    def pass_x(w, u, shift):
        f = (w[0] * rolled(u, 1, 1) + w[1] * u + w[2] * rolled(u, -1, 1)
             + w[3] * rolled(u, -2, 1))
        return choose(shift, (rolled(f, 2, 1), rolled(f, 1, 1), f, rolled(f, -1, 1)))

    def edges(step, source, start):
        w = cubic_weights(fractions[step, 0])
        first, last = pl.ds(0, EDGE), pl.ds(rows - EDGE, EDGE)
        for z in range(depth):
            value = pass_x(
                w, jnp.concatenate([source[z, first, :], source[z, last, :]], axis=0),
                jnp.concatenate([shifts[step, 0, z, first, :], shifts[step, 0, z, last, :]],
                                axis=0))
            ypad[z, pl.ds(8, EDGE), :] = value[:EDGE, :]
            ypad[z, pl.ds(8 + rows - EDGE, EDGE), :] = value[EDGE:, :]
            ysend[step, 0, pl.ds(z * EDGE, EDGE), :] = value[EDGE:, :]
            ysend[step, 1, pl.ds(z * EDGE, EDGE), :] = value[:EDGE, :]
            if start and z % per == per - 1:
                for c in y_copies(step, z // per):
                    c.start()

    def rest(step, source, last):
        halo = HALO + 1 if last else HALO
        w_x = cubic_weights(fractions[step, 0])
        middle = pl.ds(EDGE, rows - 2 * EDGE)
        for z in range(depth):
            ypad[z, pl.ds(8 + EDGE, rows - 2 * EDGE), :] = pass_x(
                w_x, source[z, middle, :], shifts[step, 0, z, middle, :])
        w = cubic_weights(fractions[step, 1])

        def pass_y(part, z):
            for start, count, at in part[0]:
                f = w[0] * ypad[z, pl.ds(5 + start, count + 3), :]
                for n in range(1, 4):
                    f = f + w[n] * ypad[z, pl.ds(5 + start + n, count + 3), :]
                yf[z, pl.ds(0, count + 3), :] = f
                part[1][step, z, pl.ds(at, count), :] = choose(
                    shifts[step, 1, z, pl.ds(start, count), :],
                    [yf[z, pl.ds(o, count), :] for o in range(4)])

        for z in range(depth):
            pass_y(inner, z)
        start_z(step, inner, halo)
        for z in range(depth):
            if z % per == 0:
                for c in y_copies(step, z // per):
                    c.wait_recv()
            take_edges(step, z)
            if last:
                for m in range(7):
                    rim_rows[m, pl.ds(2 * z, 1), :] = ypad[z, pl.ds(4 + m, 1), :]
                    rim_rows[m, pl.ds(2 * z + 1, 1), :] = ypad[z, pl.ds(5 + rows + m, 1), :]
            pass_y(outer, z)
        if last:
            for c in ahead:
                c.wait_recv()
            odd = lax.broadcasted_iota(jnp.int32, (2 * depth, width), 0) % 2 == 1

            def rim_shift(at):
                part = pl.ds(at, 2 * depth)
                return jnp.where(odd, yshift[1, part, :], yshift[0, part, :])

            rim[mine, :] = choose(rim_shift(2 * depth), [
                w[0] * rim_rows[o] + w[1] * rim_rows[o + 1] + w[2] * rim_rows[o + 2]
                + w[3] * rim_rows[o + 3] for o in range(4)])
            for c in rim_copies():
                c.start()
        start_z(step, outer, halo)
        w_z = cubic_weights(fractions[step, 2])

        def pass_z(part):
            pieces, mid, received, _ = part
            for c in z_copies(step, part, halo):
                c.wait_recv()
            size = sum(count for _, count, _ in pieces)

            def layer(k):
                if k < 0:
                    return received[step, 0, halo + k]
                if k < depth:
                    return mid[step, k]
                return received[step, 1, k - depth]

            low = 1 - halo
            for k in range(low, depth + halo - 2):
                zf[k - low, pl.ds(0, size), :] = (w_z[0] * layer(k - 1) + w_z[1] * layer(k)
                                                  + w_z[2] * layer(k + 1) + w_z[3] * layer(k + 2))
            for z in range(-1, depth + 1) if last else range(depth):
                for start, count, at in pieces:
                    part = pl.ds(start, count)
                    options = [zf[z + o - 2 - low, pl.ds(at, count), :] for o in range(4)]
                    if z < 0:
                        beyond[0, part, :] = choose(zshift[0, part, :], options)
                    elif z == depth:
                        beyond[1, part, :] = choose(zshift[1, part, :], options)
                    else:
                        img[z, part, :] = choose(shifts[step, 2, z, part, :], options)

        pass_z(inner)
        if last:
            for c in rim_copies():
                c.wait_recv()
            span = 2 * (depth + 3)
            f = w_z[0] * rim[pl.ds(2 * depth - 6, span), :]
            for n in range(1, 4):
                f = f + w_z[n] * rim[pl.ds(2 * depth - 6 + 2 * n, span), :]
            rim_f[...] = f
            value = choose(rim_shift(0), [rim_f[pl.ds(2 * o, 2 * depth), :] for o in range(4)])
            for z in range(depth):
                ypad[z, pl.ds(7, 1), :] = value[2 * z:2 * z + 1, :]
                ypad[z, pl.ds(8 + rows, 1), :] = value[2 * z + 1:2 * z + 2, :]
        pass_z(outer)
        for chunk in range(chunks):
            for c in y_copies(step, chunk):
                c.wait_send()
        for part in (inner, outer):
            for c in z_copies(step, part, halo):
                c.wait_send()
        if last:
            for c in ahead + rim_copies():
                c.wait_send()

    def advance(step, carry):
        rest(step, img, False)
        edges(step + 1, img, True)
        return carry

    fetches[0].wait()
    fetch_shifts(0).wait()
    edges(0, template, False)
    for z in range(depth):
        img[z] = template[z]
    for step in range(1, steps):
        fetch_shifts(step).wait()
    for place, kind in enumerate((2, 1)):
        for z in range(depth):
            for side, row in enumerate((rows - 1, 0)):
                value = shifts[steps - 1, kind, z, pl.ds(row, 1), :]
                for twin in range(2):
                    yshift_send[side, pl.ds(2 * (place * depth + z) + twin, 1), :] = value
    mixed[...] = jnp.zeros_like(mixed)
    pl.semaphore_wait(barrier, ny + nz - 2)
    for chunk in range(chunks):
        for c in y_copies(0, chunk):
            c.start()
    for c in ahead:
        c.start()
    lax.fori_loop(0, steps - 1, advance, 0)
    rest(steps - 1, img, True)

    fetches[1].wait()
    for z in range(depth):
        u = img[z]
        deformed[z] = u
        ypad[z, pl.ds(8, rows), :] = u
        mismatch = u - target[z]
        forces[pl.ds(z * rows, rows), :] = (
            mismatch * ((rolled(u, -1, 1) - rolled(u, 1, 1)) * 0.5))
        grad = (ypad[z, pl.ds(9, rows), :] - ypad[z, pl.ds(7, rows), :]) * 0.5
        forces[pl.ds((depth + z) * rows, rows), :] = mismatch * grad
        above = img[z + 1] if z + 1 < depth else beyond[1]
        below = img[z - 1] if z > 0 else beyond[0]
        forces[pl.ds((2 * depth + z) * rows, rows), :] = mismatch * ((above - below) * 0.5)

    dc, rc, wc = depth // 2, rows // 2, width // 2
    for c in range(3):
        for z in range(dc):
            base = (c * depth + 2 * z) * rows
            zsum[pl.ds((c * dc + z) * rows, rows), :] = (
                forces[pl.ds(base, rows), :] + forces[pl.ds(base + rows, rows), :])
    for i in (7, 8, 11):
        fetches[i].wait()
    f32dot = functools.partial(jnp.dot, preferred_element_type=jnp.float32)
    high, low = split(zsum[...])
    high, low = split(dot3(high, low, fold_hi[...], fold_lo[...]))
    coarse[0] = f32dot(pair_y[...], high) + f32dot(pair_y[...], low)
    gathers = []
    for k in range(nz - 1):
        away = jnp.where(me_z < nz // 2, nz - 1 - k, k)
        away = away + jnp.where(me_z < nz // 2, -(away <= me_z).astype(jnp.int32),
                                (away >= me_z).astype(jnp.int32))
        slot = lax.rem(me_z - away + nz, nz)
        gathers.append(copy(coarse.at[0], coarse.at[slot], cs_send.at[slot - 1],
                            cs_recv.at[slot - 1], (me_y, away)))
    for c in gathers:
        c.start()

    for i in (3, 4, 5):
        fetches[i].wait()
    high, low = split(forces[...])
    ghat[...] = dot3(high, low, hart_hi[...], hart_lo[...])
    for k in range(cz):
        g = ghat[pl.ds(k * rows, rows), :]
        msend[pl.ds(k, 1), :] = jnp.sum(g * tables[0], axis=0, keepdims=True)
        msend[pl.ds(cz + k, 1), :] = jnp.sum(g * tables[1], axis=0, keepdims=True)
    moments = [copy(msend, mrecv.at[d - 1], ms_send.at[d - 1], ms_recv.at[d - 1], at_y(d))
               for d in range(1, ny)]
    for c in moments:
        c.start()
    fetches[13].wait()
    for d in range(1, nz):
        copy(coarse.at[0], coarse.at[d], cs_send.at[d - 1], cs_recv.at[d - 1], at_z(-d)).wait()
    total, far = nz * dc, far_layers(nz * dc)
    lanes = min(wc, 128)
    for c in range(3):
        for h in range(wc // lanes):
            across = pl.ds(h * lanes, lanes)

            def level(z, c=c, across=across):
                return coarse[z % total // dc, pl.ds((c * dc + z % dc) * rc, rc), across]

            for a in range(dc):
                for dz in range(far):
                    value = level(a + dz)
                    if 0 < dz and 2 * dz != total:
                        value = value + level(a + total - dz)
                    mixed[h, a * far + dz, pl.ds(rc, rc), :] = value
            for a in range(dc):
                sums = [None] * 3

                def add(side, value):
                    sums[side] = value if sums[side] is None else sums[side] + value

                row = 0
                for dz in range(far):
                    for dy in range(CHEB - dz):
                        tap = taps[pl.ds(row, 1), across]
                        row += 1
                        at = [mixed[h, a * far + dz, pl.ds(o, rc), :]
                              for o in (dy, rc - dy, rc + dy, 2 * rc - dy)]
                        if dy == 0:
                            add(0, tap * at[1])
                        else:
                            add(0, tap * (at[1] + at[2]))
                            add(1, tap * at[0])
                            add(2, tap * at[3])
                for side in range(3):
                    parts[side, pl.ds((c * dc + a) * rc, rc), across] = sums[side]
    sides = [copy(parts.at[1], arrived.at[0], hs_send.at[0], hs_recv.at[0], at_y(-1)),
             copy(parts.at[2], arrived.at[1], hs_send.at[1], hs_recv.at[1], at_y(1))]
    for c in sides:
        c.start()
    for c in moments:
        c.wait()
    fetches[6].wait()
    from_left = hops[pl.ds(ny - 1, 1), :] * msend[pl.ds(0, cz), :]
    from_right = hops[pl.ds(ny - 1, 1), :] * msend[pl.ds(cz, cz), :]
    for m in range(1, ny):
        from_left = from_left + hops[pl.ds(m - 1, 1), :] * mrecv[m - 1, pl.ds(0, cz), :]
        from_right = from_right + hops[pl.ds(m - 1, 1), :] * mrecv[ny - m - 1, pl.ds(cz, cz), :]
    levels = (tables.shape[0] - 5) // 2
    for k in range(cz):
        g = ghat[pl.ds(k * rows, rows), :]
        down, up = g, g
        for level in range(levels):
            down = down + tables[5 + level] * rolled(down, 1 << level, 0)
            up = up + tables[5 + levels + level] * rolled(up, -(1 << level), 0)
        s = (tables[4] * (down + (up - g)) + tables[2] * from_left[k:k + 1, :]
             + tables[3] * from_right[k:k + 1, :])
        high, low = split(s)
        fhi[pl.ds(k * rows, rows), :] = high
        flo[pl.ds(k * rows, rows), :] = low
    ghat[...] = dot3(fhi[...], flo[...], hart_hi[...], hart_lo[...])

    for i in (9, 10, 12):
        fetches[i].wait()
    for c in sides:
        c.wait()
    high, low = split(parts[0] + (arrived[0] + arrived[1]))
    tall = f32dot(spread_y[...], high) + f32dot(spread_y[...], low)
    high, low = split(tall)
    zsum[...] = dot3(high, low, spread_hi[...], spread_lo[...])
    for c in range(3):
        for z in range(depth):
            fine = zsum[pl.ds((c * dc + z // 2) * rows, rows), :]
            update[c, z] = -(ghat[pl.ds((c * depth + z) * rows, rows), :] + fine)


def on_device(template, target, shifts, fractions, *, ny, nz):
    depth, rows, width = template.shape
    steps = shifts.shape[0]
    dc, rc, wc = depth // 2, rows // 2, width // 2
    cz = 3 * depth
    hart_hi, hart_lo, tables, hops = make_tables(rows, width, ny)
    fold_hi, fold_lo, spread_hi, spread_lo, taps = make_coarse(width, nz * dc, ny * rc)
    pair_y = np.kron(np.eye(3 * dc * rc), np.ones((1, 2))).astype(jnp.bfloat16)
    spread_y = np.ascontiguousarray(pair_y.T)
    f32, bf16 = jnp.float32, jnp.bfloat16
    vmem, dma = pltpu.VMEM, pltpu.SemaphoreType.DMA
    scratch = [
        vmem((depth, rows, width), f32),
        vmem((depth, rows + 16, width), f32),
        vmem((depth, rows + 8, width), f32),
        vmem((steps, 2, depth * EDGE, width), f32),
        vmem((steps, 2, depth * EDGE, width), f32),
        vmem((steps, depth, rows - 2 * EDGE, width), f32),
        vmem((steps, 2, HALO + 1, rows - 2 * EDGE, width), f32),
        vmem((steps, depth, 2 * EDGE, width), f32),
        vmem((steps, 2, HALO + 1, 2 * EDGE, width), f32),
        vmem((depth + 5, rows, width), f32),
        vmem((2, rows, width), f32),
        vmem((2, rows, width), shifts.dtype),
        vmem((2, 4 * depth, width), shifts.dtype),
        vmem((2, 4 * depth, width), shifts.dtype),
        vmem((6 * depth, width), f32),
        vmem((7, 2 * depth, width), f32),
        vmem((2 * (depth + 3), width), f32),
        vmem((cz * rows, width), f32),
        vmem((cz * rows, width), f32),
        vmem((2 * cz, width), f32),
        vmem((ny - 1, 2 * cz, width), f32),
        vmem((nz, 3 * dc * rc, wc), f32),
        vmem((3, 3 * dc * rc, wc), f32),
        vmem((2, 3 * dc * rc, wc), f32),
        vmem((-(-wc // 128), dc * far_layers(nz * dc), 3 * rc, min(wc, 128)), f32),
        vmem((3 * dc * rows, width), f32),
        vmem((cz * rows, width), bf16),
        vmem((cz * rows, width), bf16),
        dma((steps, 2, depth * EDGE // 8)), dma((steps, 2, depth * EDGE // 8)),
        dma((steps, 2, 2)), dma((steps, 2, 2)),
        dma((2,)), dma((2,)), dma((2,)), dma((2,)), dma((2,)), dma((2,)),
        dma((ny - 1,)), dma((ny - 1,)),
        dma((nz - 1,)), dma((nz - 1,)),
        dma((2,)), dma((2,)),
    ]
    spec = pl.BlockSpec(memory_space=pltpu.VMEM)
    smem = pl.BlockSpec(memory_space=pltpu.SMEM)
    hbm = pl.BlockSpec(memory_space=pltpu.HBM)
    operands = [template, target, shifts, jnp.asarray(hart_hi), jnp.asarray(hart_lo),
                *map(jnp.asarray, (tables, hops, fold_hi, fold_lo, spread_hi, spread_lo, pair_y,
                                   spread_y, taps))]
    held = [vmem(x.shape, x.dtype) for x in operands]
    scratch = held + [dma((len(operands),)), dma((steps,))] + scratch
    return tuple(pl.pallas_call(
        functools.partial(kernel, ny, nz),
        out_shape=(vmem((3, depth, rows, width), f32), vmem((depth, rows, width), f32)),
        in_specs=[smem] + [hbm] * len(operands),
        out_specs=(spec, spec),
        scratch_shapes=scratch,
        compiler_params=pltpu.CompilerParams(
            collective_id=0, has_side_effects=True),
    )(fractions, *operands))


def solution(mesh):
    return jax.shard_map(
        functools.partial(on_device, ny=mesh.shape["gy"], nz=mesh.shape["gz"]),
        mesh=mesh,
        in_specs=(P("gz", "gy", None), P("gz", "gy", None), P(None, None, "gz", "gy", None), P()),
        out_specs=(P(None, "gz", "gy", None), P("gz", "gy", None)),
        check_vma=False,
    )
```

```python
import functools

import jax
import jax.numpy as jnp
import numpy as np
from jax import lax
from jax.experimental import pallas as pl
from jax.experimental.pallas import tpu as pltpu
from jax.sharding import PartitionSpec as P

CHEB = 8
DAMPING = 0.25
ACROSS_WEIGHT = 0.0625
ALONG_SCALE = 32.0
SHIFT = 0.25
MESH = pl.DeviceIdType.MESH
EDGE = 4
HALO = 3


def cubic_weights(fraction):
    return (
        -fraction * (fraction - 1.0) * (fraction - 2.0) / 6.0,
        (fraction + 1.0) * (fraction - 1.0) * (fraction - 2.0) / 2.0,
        -(fraction + 1.0) * fraction * (fraction - 2.0) / 2.0,
        (fraction + 1.0) * fraction * (fraction - 1.0) / 6.0,
    )


def turn_factors(count):
    low, high = SHIFT, SHIFT + 12.0
    theta, delta = (high + low) / 2.0, (high - low) / 2.0
    sigma = theta / delta
    now = 1.0 / sigma
    factors = []
    for _ in range(count - 1):
        after = 1.0 / (2.0 * sigma - now)
        factors.append((after * now, 2.0 * after / delta))
        now = after
    return theta, factors


def make_tables(rows, length_x, peers):
    length_y = rows * peers
    index = np.arange(length_x)
    angle = 2.0 * np.pi / length_x * (np.outer(index, index) % length_x)
    hartley = np.cos(angle) + np.sin(angle)
    weight = (length_y / ALONG_SCALE) ** 2
    a = DAMPING + 4.0 * ACROSS_WEIGHT * np.sin(np.pi * index / length_x) ** 2
    half = a / (2.0 * weight)
    r = 1.0 / (1.0 + half + np.sqrt(half * (half + 2.0)))
    y = np.arange(rows)[:, None]
    scale = 1.0 / (weight * (1.0 / r - r) * length_x)
    down, up, stride = [], [], 1
    while stride < rows:
        down.append(np.where(y >= stride, r ** stride, 0.0))
        up.append(np.where(y < rows - stride, r ** stride, 0.0))
        stride *= 2
    tables = [r ** (rows - 1 - y), r ** y, scale * r ** (y + 1), scale * r ** (rows - y),
              scale + 0.0 * r * y] + down + up
    m = np.arange(peers)[:, None]
    hops = r ** (rows * m) / (1.0 - r ** length_y)
    high = hartley.astype(jnp.bfloat16)
    low = (hartley - high.astype(np.float64)).astype(jnp.bfloat16)
    return high, low, np.stack(tables).astype(np.float32), hops.astype(np.float32)


def cas(length):
    index = np.arange(length)
    angle = 2.0 * np.pi / length * (np.outer(index, index) % length)
    return np.cos(angle) + np.sin(angle)


def in_two(table):
    high = table.astype(jnp.bfloat16)
    return high, (table - high.astype(np.float64)).astype(jnp.bfloat16)


def far_layers(total):
    return min(total // 2, CHEB - 1) + 1


def make_coarse(width, total, length_y):
    half = width // 2
    pair = np.kron(np.eye(half), np.full((2, 1), 0.125))
    fold = in_two(pair @ cas(half))
    spread = in_two(cas(half) @ np.kron(np.eye(half), np.ones((1, 2))) / half)
    x, y, z = [2.0 * np.cos(2.0 * np.pi * np.arange(n) / n) for n in (half, length_y, total)]
    symbol = SHIFT + 6.0 - (z[:, None, None] + y[None, :, None] + x[None, None, :])
    theta, factors = turn_factors(CHEB)
    residual = np.ones_like(symbol)
    direction = residual / theta
    gain = direction
    for keep, add in factors:
        residual = residual - symbol * direction
        direction = keep * direction + add * residual
        gain = gain + direction
    taps = []
    for dz in range(far_layers(total)):
        in_z = np.cos(2.0 * np.pi * dz * np.arange(total) / total) / total
        plane = np.tensordot(in_z, gain, 1)
        for dy in range(CHEB - dz):
            in_y = np.cos(2.0 * np.pi * dy * np.arange(length_y) / length_y) / length_y
            taps.append(in_y @ plane)
    return fold + spread + (np.stack(taps).astype(np.float32),)


def dot3(high, low, table_high, table_low):
    f = functools.partial(jnp.dot, preferred_element_type=jnp.float32)
    return f(high, table_high) + (f(low, table_high) + f(high, table_low))


def split(value):
    high = value.astype(jnp.bfloat16)
    return high, (value - high.astype(jnp.float32)).astype(jnp.bfloat16)


def choose(shift, options):
    minus2, minus1, zero, one = options
    result = jnp.where(shift == 0, zero, one)
    result = jnp.where(shift == -1, minus1, result)
    return jnp.where(shift == -2, minus2, result)


def kernel(ny, nz, *refs):
    me_y, me_z = lax.axis_index("gy"), lax.axis_index("gz")
    barrier = pltpu.get_barrier_semaphore()
    for d in range(1, ny):
        pl.semaphore_signal(barrier, inc=1, device_id=(lax.rem(me_y + d, ny), me_z),
                            device_id_type=MESH)
    for d in range(1, nz):
        pl.semaphore_signal(barrier, inc=1, device_id=(me_y, lax.rem(me_z + d, nz)),
                            device_id_type=MESH)
    count = 15
    sources, (update, deformed), rest = refs[:count], refs[count:count + 2], refs[count + 2:]
    held, fetch_sems, shift_sems = rest[:count], rest[count], rest[count + 1]
    step_count = held[2].shape[0]
    fetches = {}
    for i in (0, 1, *range(3, count)):
        fetches[i] = pltpu.make_async_copy(sources[i], held[i], fetch_sems.at[i])

    def fetch_shifts(step):
        return pltpu.make_async_copy(sources[2].at[step], held[2].at[step], shift_sems.at[step])

    fetches[0].start()
    fetches[14].start()
    for step in range(step_count):
        fetch_shifts(step).start()
    for i in (1, 7, 8, 11, 3, 4, 5, 6, 13, 9, 10, 12):
        fetches[i].start()
    body(ny, nz, held[14], fetches, fetch_shifts, sources[2], *held[:14], update, deformed, *rest[count + 2:])


def body(ny, nz, fractions, fetches, fetch_shifts, all_shifts, template, target, shifts, hart_hi, hart_lo,
         tables, hops, fold_hi, fold_lo, spread_hi, spread_lo, pair_y, spread_y, taps,
         update, deformed, img, ypad, yf, ysend, yrecv, zmid, zrecv, zmid_edge, zrecv_edge,
           zf, beyond, zshift, yshift_send, yshift, rim, rim_rows, rim_f, forces, ghat, msend, mrecv, coarse, parts, arrived, mixed,
           zsum, fhi, flo, ys_send, ys_recv, zs_send, zs_recv, rs_send, rs_recv, zh_send, zh_recv, yh_send, yh_recv, ms_send, ms_recv,
           cs_send, cs_recv, hs_send, hs_recv):
    depth, rows, width = template.shape
    steps = shifts.shape[0]
    cz = 3 * depth
    me_y, me_z = lax.axis_index("gy"), lax.axis_index("gz")

    def at_y(offset):
        return (lax.rem(me_y + (offset + ny), ny), me_z)

    def at_z(offset):
        return (me_y, lax.rem(me_z + (offset + nz), nz))

    def copy(src, dst, send, recv, device):
        return pltpu.make_async_remote_copy(
            src_ref=src, dst_ref=dst, send_sem=send, recv_sem=recv, device_id=device,
            device_id_type=MESH)

    def rolled(value, by, axis):
        return pltpu.roll(value, by % value.shape[axis], axis)

    chunks = depth * EDGE // 8
    per = depth // chunks

    def y_copies(step, chunk):
        part = pl.ds(chunk * 8, 8)
        return [copy(ysend.at[step, side, part], yrecv.at[step, side, part],
                     ys_send.at[step, side, chunk], ys_recv.at[step, side, chunk],
                     at_y(1 - 2 * side)) for side in range(2)]

    inner = (((EDGE, rows - 2 * EDGE, 0),), zmid, zrecv, 0)
    outer = (((0, EDGE, 0), (rows - EDGE, EDGE, EDGE)), zmid_edge, zrecv_edge, 1)

    def z_copies(step, part, halo=HALO, side=None):
        _, mid, received, which = part
        if side is None:
            return [z_copies(step, part, halo, side) for side in range(2)]
        return copy(mid.at[step, pl.ds((1 - side) * (depth - halo), halo)],
                    received.at[step, side, pl.ds(0, halo)], zs_send.at[step, side, which],
                    zs_recv.at[step, side, which], at_z(1 - 2 * side))

    far_side = jnp.where(me_z < nz // 2, 1, 0)

    def start_z(step, part, halo=HALO):
        for side in (far_side, 1 - far_side):
            z_copies(step, part, halo, side).start()

    mine = pl.ds(2 * depth, 2 * depth)

    def rim_copies():
        return [copy(rim.at[mine], rim.at[pl.ds(side * 4 * depth, 2 * depth)],
                     rs_send.at[side], rs_recv.at[side], at_z(1 - 2 * side)) for side in range(2)]

    ahead = [copy(all_shifts.at[steps - 1, 2, depth - 1], zshift.at[0], zh_send.at[0],
                  zh_recv.at[0], at_z(1)),
             copy(all_shifts.at[steps - 1, 2, 0], zshift.at[1], zh_send.at[1], zh_recv.at[1],
                  at_z(-1)),
             copy(yshift_send.at[0], yshift.at[0], yh_send.at[0], yh_recv.at[0], at_y(1)),
             copy(yshift_send.at[1], yshift.at[1], yh_send.at[1], yh_recv.at[1], at_y(-1))]

    def take_edges(step, z):
        ypad[z, pl.ds(8 - EDGE, EDGE), :] = yrecv[step, 0, pl.ds(z * EDGE, EDGE), :]
        ypad[z, pl.ds(8 + rows, EDGE), :] = yrecv[step, 1, pl.ds(z * EDGE, EDGE), :]

    def pass_x(w, u, shift):
        f = (w[0] * rolled(u, 1, 1) + w[1] * u + w[2] * rolled(u, -1, 1)
             + w[3] * rolled(u, -2, 1))
        return choose(shift, (rolled(f, 2, 1), rolled(f, 1, 1), f, rolled(f, -1, 1)))

    def edges(step, source, start):
        w = cubic_weights(fractions[step, 0])
        first, last = pl.ds(0, EDGE), pl.ds(rows - EDGE, EDGE)
        for z in range(depth):
            value = pass_x(
                w, jnp.concatenate([source[z, first, :], source[z, last, :]], axis=0),
                jnp.concatenate([shifts[step, 0, z, first, :], shifts[step, 0, z, last, :]],
                                axis=0))
            ypad[z, pl.ds(8, EDGE), :] = value[:EDGE, :]
            ypad[z, pl.ds(8 + rows - EDGE, EDGE), :] = value[EDGE:, :]
            ysend[step, 0, pl.ds(z * EDGE, EDGE), :] = value[EDGE:, :]
            ysend[step, 1, pl.ds(z * EDGE, EDGE), :] = value[:EDGE, :]
            if start and z % per == per - 1:
                for c in y_copies(step, z // per):
                    c.start()

    def rest(step, source, last):
        halo = HALO + 1 if last else HALO
        w_x = cubic_weights(fractions[step, 0])
        middle = pl.ds(EDGE, rows - 2 * EDGE)
        for z in range(depth):
            ypad[z, pl.ds(8 + EDGE, rows - 2 * EDGE), :] = pass_x(
                w_x, source[z, middle, :], shifts[step, 0, z, middle, :])
        w = cubic_weights(fractions[step, 1])

        def pass_y(part, z):
            for start, count, at in part[0]:
                f = w[0] * ypad[z, pl.ds(5 + start, count + 3), :]
                for n in range(1, 4):
                    f = f + w[n] * ypad[z, pl.ds(5 + start + n, count + 3), :]
                yf[z, pl.ds(0, count + 3), :] = f
                part[1][step, z, pl.ds(at, count), :] = choose(
                    shifts[step, 1, z, pl.ds(start, count), :],
                    [yf[z, pl.ds(o, count), :] for o in range(4)])

        for z in range(depth):
            pass_y(inner, z)
        start_z(step, inner, halo)
        for z in range(depth):
            if z % per == 0:
                for c in y_copies(step, z // per):
                    c.wait_recv()
            take_edges(step, z)
            if last:
                for m in range(7):
                    rim_rows[m, pl.ds(2 * z, 1), :] = ypad[z, pl.ds(4 + m, 1), :]
                    rim_rows[m, pl.ds(2 * z + 1, 1), :] = ypad[z, pl.ds(5 + rows + m, 1), :]
            pass_y(outer, z)
        if last:
            for c in ahead:
                c.wait_recv()
            odd = lax.broadcasted_iota(jnp.int32, (2 * depth, width), 0) % 2 == 1

            def rim_shift(at):
                part = pl.ds(at, 2 * depth)
                return jnp.where(odd, yshift[1, part, :], yshift[0, part, :])

            rim[mine, :] = choose(rim_shift(2 * depth), [
                w[0] * rim_rows[o] + w[1] * rim_rows[o + 1] + w[2] * rim_rows[o + 2]
                + w[3] * rim_rows[o + 3] for o in range(4)])
            for c in rim_copies():
                c.start()
        start_z(step, outer, halo)
        w_z = cubic_weights(fractions[step, 2])

        def pass_z(part):
            pieces, mid, received, _ = part
            for c in z_copies(step, part, halo):
                c.wait_recv()
            size = sum(count for _, count, _ in pieces)

            def layer(k):
                if k < 0:
                    return received[step, 0, halo + k]
                if k < depth:
                    return mid[step, k]
                return received[step, 1, k - depth]

            low = 1 - halo
            for k in range(low, depth + halo - 2):
                zf[k - low, pl.ds(0, size), :] = (w_z[0] * layer(k - 1) + w_z[1] * layer(k)
                                                  + w_z[2] * layer(k + 1) + w_z[3] * layer(k + 2))
            for z in range(-1, depth + 1) if last else range(depth):
                for start, count, at in pieces:
                    part = pl.ds(start, count)
                    options = [zf[z + o - 2 - low, pl.ds(at, count), :] for o in range(4)]
                    if z < 0:
                        beyond[0, part, :] = choose(zshift[0, part, :], options)
                    elif z == depth:
                        beyond[1, part, :] = choose(zshift[1, part, :], options)
                    else:
                        img[z, part, :] = choose(shifts[step, 2, z, part, :], options)

        pass_z(inner)
        if last:
            for c in rim_copies():
                c.wait_recv()
            span = 2 * (depth + 3)
            f = w_z[0] * rim[pl.ds(2 * depth - 6, span), :]
            for n in range(1, 4):
                f = f + w_z[n] * rim[pl.ds(2 * depth - 6 + 2 * n, span), :]
            rim_f[...] = f
            value = choose(rim_shift(0), [rim_f[pl.ds(2 * o, 2 * depth), :] for o in range(4)])
            for z in range(depth):
                ypad[z, pl.ds(7, 1), :] = value[2 * z:2 * z + 1, :]
                ypad[z, pl.ds(8 + rows, 1), :] = value[2 * z + 1:2 * z + 2, :]
        pass_z(outer)
        for chunk in range(chunks):
            for c in y_copies(step, chunk):
                c.wait_send()
        for part in (inner, outer):
            for c in z_copies(step, part, halo):
                c.wait_send()
        if last:
            for c in ahead + rim_copies():
                c.wait_send()

    def advance(step, carry):
        rest(step, img, False)
        edges(step + 1, img, True)
        return carry

    fetches[14].wait()
    fetches[0].wait()
    fetch_shifts(0).wait()
    edges(0, template, False)
    for z in range(depth):
        img[z] = template[z]
    for step in range(1, steps):
        fetch_shifts(step).wait()
    for place, kind in enumerate((2, 1)):
        for z in range(depth):
            for side, row in enumerate((rows - 1, 0)):
                value = shifts[steps - 1, kind, z, pl.ds(row, 1), :]
                for twin in range(2):
                    yshift_send[side, pl.ds(2 * (place * depth + z) + twin, 1), :] = value
    mixed[...] = jnp.zeros_like(mixed)
    pl.semaphore_wait(pltpu.get_barrier_semaphore(), ny + nz - 2)
    for chunk in range(chunks):
        for c in y_copies(0, chunk):
            c.start()
    for c in ahead:
        c.start()
    lax.fori_loop(0, steps - 1, advance, 0)
    rest(steps - 1, img, True)

    fetches[1].wait()
    for z in range(depth):
        u = img[z]
        deformed[z] = u
        ypad[z, pl.ds(8, rows), :] = u
        mismatch = u - target[z]
        forces[pl.ds(z * rows, rows), :] = (
            mismatch * ((rolled(u, -1, 1) - rolled(u, 1, 1)) * 0.5))
        grad = (ypad[z, pl.ds(9, rows), :] - ypad[z, pl.ds(7, rows), :]) * 0.5
        forces[pl.ds((depth + z) * rows, rows), :] = mismatch * grad
        above = img[z + 1] if z + 1 < depth else beyond[1]
        below = img[z - 1] if z > 0 else beyond[0]
        forces[pl.ds((2 * depth + z) * rows, rows), :] = mismatch * ((above - below) * 0.5)

    dc, rc, wc = depth // 2, rows // 2, width // 2
    for c in range(3):
        for z in range(dc):
            base = (c * depth + 2 * z) * rows
            zsum[pl.ds((c * dc + z) * rows, rows), :] = (
                forces[pl.ds(base, rows), :] + forces[pl.ds(base + rows, rows), :])
    for i in (7, 8, 11):
        fetches[i].wait()
    f32dot = functools.partial(jnp.dot, preferred_element_type=jnp.float32)
    high, low = split(zsum[...])
    high, low = split(dot3(high, low, fold_hi[...], fold_lo[...]))
    coarse[0] = f32dot(pair_y[...], high) + f32dot(pair_y[...], low)
    gathers = []
    for k in range(nz - 1):
        away = jnp.where(me_z < nz // 2, nz - 1 - k, k)
        away = away + jnp.where(me_z < nz // 2, -(away <= me_z).astype(jnp.int32),
                                (away >= me_z).astype(jnp.int32))
        slot = lax.rem(me_z - away + nz, nz)
        gathers.append(copy(coarse.at[0], coarse.at[slot], cs_send.at[slot - 1],
                            cs_recv.at[slot - 1], (me_y, away)))
    for c in gathers:
        c.start()

    for i in (3, 4, 5):
        fetches[i].wait()
    high, low = split(forces[...])
    ghat[...] = dot3(high, low, hart_hi[...], hart_lo[...])
    for k in range(cz):
        g = ghat[pl.ds(k * rows, rows), :]
        msend[pl.ds(k, 1), :] = jnp.sum(g * tables[0], axis=0, keepdims=True)
        msend[pl.ds(cz + k, 1), :] = jnp.sum(g * tables[1], axis=0, keepdims=True)
    moments = [copy(msend, mrecv.at[d - 1], ms_send.at[d - 1], ms_recv.at[d - 1], at_y(d))
               for d in range(1, ny)]
    for d in sorted(range(1, ny), key=lambda d: -min(d, ny - d)):
        moments[d - 1].start()
    levels = (tables.shape[0] - 5) // 2
    for k in range(cz):
        g = ghat[pl.ds(k * rows, rows), :]
        down, up = g, g
        for level in range(levels):
            down = down + tables[5 + level] * rolled(down, 1 << level, 0)
            up = up + tables[5 + levels + level] * rolled(up, -(1 << level), 0)
        ghat[pl.ds(k * rows, rows), :] = tables[4] * (down + (up - g))
    fetches[13].wait()
    for d in range(1, nz):
        copy(coarse.at[0], coarse.at[d], cs_send.at[d - 1], cs_recv.at[d - 1], at_z(-d)).wait()
    sides = [[copy(parts.at[1 + side, pl.ds(c * dc * rc, dc * rc)],
                   arrived.at[side, pl.ds(c * dc * rc, dc * rc)], hs_send.at[side, c],
                   hs_recv.at[side, c], at_y(2 * side - 1)) for side in range(2)]
             for c in range(3)]
    total, far = nz * dc, far_layers(nz * dc)
    lanes = min(wc, 128)
    for c in range(3):
        for h in range(wc // lanes):
            across = pl.ds(h * lanes, lanes)

            def level(z, c=c, across=across):
                return coarse[z % total // dc, pl.ds((c * dc + z % dc) * rc, rc), across]

            for a in range(dc):
                for dz in range(far):
                    value = level(a + dz)
                    if 0 < dz and 2 * dz != total:
                        value = value + level(a + total - dz)
                    mixed[h, a * far + dz, pl.ds(rc, rc), :] = value
            for a in range(dc):
                sums = [None] * 3

                def add(side, value):
                    sums[side] = value if sums[side] is None else sums[side] + value

                row = 0
                for dz in range(far):
                    for dy in range(CHEB - dz):
                        tap = taps[pl.ds(row, 1), across]
                        row += 1
                        at = [mixed[h, a * far + dz, pl.ds(o, rc), :]
                              for o in (dy, rc - dy, rc + dy, 2 * rc - dy)]
                        if dy == 0:
                            add(0, tap * at[1])
                        else:
                            add(0, tap * (at[1] + at[2]))
                            add(1, tap * at[0])
                            add(2, tap * at[3])
                for side in range(3):
                    parts[side, pl.ds((c * dc + a) * rc, rc), across] = sums[side]
        for side in sides[c]:
            side.start()
    for c in moments:
        c.wait()
    fetches[6].wait()
    from_left = hops[pl.ds(ny - 1, 1), :] * msend[pl.ds(0, cz), :]
    from_right = hops[pl.ds(ny - 1, 1), :] * msend[pl.ds(cz, cz), :]
    for m in range(1, ny):
        from_left = from_left + hops[pl.ds(m - 1, 1), :] * mrecv[m - 1, pl.ds(0, cz), :]
        from_right = from_right + hops[pl.ds(m - 1, 1), :] * mrecv[ny - m - 1, pl.ds(cz, cz), :]
    for k in range(cz):
        s = (ghat[pl.ds(k * rows, rows), :] + tables[2] * from_left[k:k + 1, :]
             + tables[3] * from_right[k:k + 1, :])
        high, low = split(s)
        fhi[pl.ds(k * rows, rows), :] = high
        flo[pl.ds(k * rows, rows), :] = low
    ghat[...] = dot3(fhi[...], flo[...], hart_hi[...], hart_lo[...])

    for i in (9, 10, 12):
        fetches[i].wait()
    for pair in sides:
        for c in pair:
            c.wait()
    high, low = split(parts[0] + (arrived[0] + arrived[1]))
    tall = f32dot(spread_y[...], high) + f32dot(spread_y[...], low)
    high, low = split(tall)
    zsum[...] = dot3(high, low, spread_hi[...], spread_lo[...])
    for c in range(3):
        for z in range(depth):
            fine = zsum[pl.ds((c * dc + z // 2) * rows, rows), :]
            update[c, z] = -(ghat[pl.ds((c * depth + z) * rows, rows), :] + fine)


def on_device(template, target, shifts, fractions, *, ny, nz):
    depth, rows, width = template.shape
    steps = shifts.shape[0]
    dc, rc, wc = depth // 2, rows // 2, width // 2
    cz = 3 * depth
    hart_hi, hart_lo, tables, hops = make_tables(rows, width, ny)
    fold_hi, fold_lo, spread_hi, spread_lo, taps = make_coarse(width, nz * dc, ny * rc)
    pair_y = np.kron(np.eye(3 * dc * rc), np.ones((1, 2))).astype(jnp.bfloat16)
    spread_y = np.ascontiguousarray(pair_y.T)
    f32, bf16 = jnp.float32, jnp.bfloat16
    vmem, dma = pltpu.VMEM, pltpu.SemaphoreType.DMA
    scratch = [
        vmem((depth, rows, width), f32),
        vmem((depth, rows + 16, width), f32),
        vmem((depth, rows + 8, width), f32),
        vmem((steps, 2, depth * EDGE, width), f32),
        vmem((steps, 2, depth * EDGE, width), f32),
        vmem((steps, depth, rows - 2 * EDGE, width), f32),
        vmem((steps, 2, HALO + 1, rows - 2 * EDGE, width), f32),
        vmem((steps, depth, 2 * EDGE, width), f32),
        vmem((steps, 2, HALO + 1, 2 * EDGE, width), f32),
        vmem((depth + 5, rows, width), f32),
        vmem((2, rows, width), f32),
        vmem((2, rows, width), shifts.dtype),
        vmem((2, 4 * depth, width), shifts.dtype),
        vmem((2, 4 * depth, width), shifts.dtype),
        vmem((6 * depth, width), f32),
        vmem((7, 2 * depth, width), f32),
        vmem((2 * (depth + 3), width), f32),
        vmem((cz * rows, width), f32),
        vmem((cz * rows, width), f32),
        vmem((2 * cz, width), f32),
        vmem((ny - 1, 2 * cz, width), f32),
        vmem((nz, 3 * dc * rc, wc), f32),
        vmem((3, 3 * dc * rc, wc), f32),
        vmem((2, 3 * dc * rc, wc), f32),
        vmem((-(-wc // 128), dc * far_layers(nz * dc), 3 * rc, min(wc, 128)), f32),
        vmem((3 * dc * rows, width), f32),
        vmem((cz * rows, width), bf16),
        vmem((cz * rows, width), bf16),
        dma((steps, 2, depth * EDGE // 8)), dma((steps, 2, depth * EDGE // 8)),
        dma((steps, 2, 2)), dma((steps, 2, 2)),
        dma((2,)), dma((2,)), dma((2,)), dma((2,)), dma((2,)), dma((2,)),
        dma((ny - 1,)), dma((ny - 1,)),
        dma((nz - 1,)), dma((nz - 1,)),
        dma((2, 3)), dma((2, 3)),
    ]
    spec = pl.BlockSpec(memory_space=pltpu.VMEM)
    hbm = pl.BlockSpec(memory_space=pltpu.HBM)
    operands = [template, target, shifts, jnp.asarray(hart_hi), jnp.asarray(hart_lo),
                *map(jnp.asarray, (tables, hops, fold_hi, fold_lo, spread_hi, spread_lo, pair_y,
                                   spread_y, taps)), fractions]
    held = [vmem(x.shape, x.dtype) for x in operands[:-1]] + [pltpu.SMEM(fractions.shape, f32)]
    scratch = held + [dma((len(operands),)), dma((steps,))] + scratch
    return tuple(pl.pallas_call(
        functools.partial(kernel, ny, nz),
        out_shape=(vmem((3, depth, rows, width), f32), vmem((depth, rows, width), f32)),
        in_specs=[hbm] * len(operands),
        out_specs=(spec, spec),
        scratch_shapes=scratch,
        compiler_params=pltpu.CompilerParams(
            collective_id=0, has_side_effects=True),
    )(*operands))


def solution(mesh):
    return jax.shard_map(
        functools.partial(on_device, ny=mesh.shape["gy"], nz=mesh.shape["gz"]),
        mesh=mesh,
        in_specs=(P("gz", "gy", None), P("gz", "gy", None), P(None, None, "gz", "gy", None), P()),
        out_specs=(P(None, "gz", "gy", None), P("gz", "gy", None)),
        check_vma=False,
    )
```

```python
import functools

import jax
import jax.numpy as jnp
import numpy as np
from jax import lax
from jax.experimental import pallas as pl
from jax.experimental.pallas import tpu as pltpu
from jax.sharding import PartitionSpec as P

CHEB = 8
DAMPING = 0.25
ACROSS_WEIGHT = 0.0625
ALONG_SCALE = 32.0
SHIFT = 0.25
MESH = pl.DeviceIdType.MESH
EDGE = 4
HALO = 3


def cubic_weights(fraction):
    return (
        -fraction * (fraction - 1.0) * (fraction - 2.0) / 6.0,
        (fraction + 1.0) * (fraction - 1.0) * (fraction - 2.0) / 2.0,
        -(fraction + 1.0) * fraction * (fraction - 2.0) / 2.0,
        (fraction + 1.0) * fraction * (fraction - 1.0) / 6.0,
    )


def turn_factors(count):
    low, high = SHIFT, SHIFT + 12.0
    theta, delta = (high + low) / 2.0, (high - low) / 2.0
    sigma = theta / delta
    now = 1.0 / sigma
    factors = []
    for _ in range(count - 1):
        after = 1.0 / (2.0 * sigma - now)
        factors.append((after * now, 2.0 * after / delta))
        now = after
    return theta, factors


def make_tables(rows, length_x, peers):
    length_y = rows * peers
    index = np.arange(length_x)
    angle = 2.0 * np.pi / length_x * (np.outer(index, index) % length_x)
    hartley = np.cos(angle) + np.sin(angle)
    weight = (length_y / ALONG_SCALE) ** 2
    a = DAMPING + 4.0 * ACROSS_WEIGHT * np.sin(np.pi * index / length_x) ** 2
    half = a / (2.0 * weight)
    r = 1.0 / (1.0 + half + np.sqrt(half * (half + 2.0)))
    y = np.arange(rows)[:, None]
    scale = 1.0 / (weight * (1.0 / r - r) * length_x)
    down, up, stride = [], [], 1
    while stride < rows:
        down.append(np.where(y >= stride, r ** stride, 0.0))
        up.append(np.where(y < rows - stride, r ** stride, 0.0))
        stride *= 2
    tables = [r ** (rows - 1 - y), r ** y, scale * r ** (y + 1), scale * r ** (rows - y),
              scale + 0.0 * r * y] + down + up
    m = np.arange(peers)[:, None]
    hops = r ** (rows * m) / (1.0 - r ** length_y)
    high = hartley.astype(jnp.bfloat16)
    low = (hartley - high.astype(np.float64)).astype(jnp.bfloat16)
    return high, low, np.stack(tables).astype(np.float32), hops.astype(np.float32)


def cas(length):
    index = np.arange(length)
    angle = 2.0 * np.pi / length * (np.outer(index, index) % length)
    return np.cos(angle) + np.sin(angle)


def in_two(table):
    high = table.astype(jnp.bfloat16)
    return high, (table - high.astype(np.float64)).astype(jnp.bfloat16)


def far_layers(total):
    return min(total // 2, CHEB - 1) + 1


def make_coarse(width, total, length_y):
    half = width // 2
    pair = np.kron(np.eye(half), np.full((2, 1), 0.125))
    fold = in_two(pair @ cas(half))
    spread = in_two(cas(half) @ np.kron(np.eye(half), np.ones((1, 2))) / half)
    x, y, z = [2.0 * np.cos(2.0 * np.pi * np.arange(n) / n) for n in (half, length_y, total)]
    symbol = SHIFT + 6.0 - (z[:, None, None] + y[None, :, None] + x[None, None, :])
    theta, factors = turn_factors(CHEB)
    residual = np.ones_like(symbol)
    direction = residual / theta
    gain = direction
    for keep, add in factors:
        residual = residual - symbol * direction
        direction = keep * direction + add * residual
        gain = gain + direction
    taps = []
    for dz in range(far_layers(total)):
        in_z = np.cos(2.0 * np.pi * dz * np.arange(total) / total) / total
        plane = np.tensordot(in_z, gain, 1)
        for dy in range(CHEB - dz):
            in_y = np.cos(2.0 * np.pi * dy * np.arange(length_y) / length_y) / length_y
            taps.append(in_y @ plane)
    return fold + spread + (np.stack(taps).astype(np.float32),)


def dot3(high, low, table_high, table_low):
    f = functools.partial(jnp.dot, preferred_element_type=jnp.float32)
    return f(high, table_high) + (f(low, table_high) + f(high, table_low))


def split(value):
    high = value.astype(jnp.bfloat16)
    return high, (value - high.astype(jnp.float32)).astype(jnp.bfloat16)


def choose(shift, options):
    minus2, minus1, zero, one = options
    result = jnp.where(shift == 0, zero, one)
    result = jnp.where(shift == -1, minus1, result)
    return jnp.where(shift == -2, minus2, result)


def kernel(ny, nz, *refs):
    me_y, me_z = lax.axis_index("gy"), lax.axis_index("gz")
    barrier = pltpu.get_barrier_semaphore()
    for d in range(1, ny):
        pl.semaphore_signal(barrier, inc=1, device_id=(lax.rem(me_y + d, ny), me_z),
                            device_id_type=MESH)
    for d in range(1, nz):
        pl.semaphore_signal(barrier, inc=1, device_id=(me_y, lax.rem(me_z + d, nz)),
                            device_id_type=MESH)
    count = 13
    sources, (update, deformed), rest = refs[:count], refs[count:count + 2], refs[count + 2:]
    held, fetch_sems, shift_sems = rest[:count], rest[count], rest[count + 1]
    step_count = held[2].shape[0]
    fetches = {}
    for i in (0, 1, *range(3, count)):
        fetches[i] = pltpu.make_async_copy(sources[i], held[i], fetch_sems.at[i])

    def fetch_shifts(step):
        return pltpu.make_async_copy(sources[2].at[step], held[2].at[step], shift_sems.at[step])

    fetches[0].start()
    fetches[12].start()
    for step in range(step_count):
        fetch_shifts(step).start()
    for i in (1, 7, 8, 3, 4, 5, 6, 11, 9, 10):
        fetches[i].start()
    body(ny, nz, held[12], fetches, fetch_shifts, sources[2], *held[:12], update, deformed, *rest[count + 2:])


def body(ny, nz, fractions, fetches, fetch_shifts, all_shifts, template, target, shifts, hart_hi, hart_lo,
         tables, hops, fold_hi, fold_lo, spread_hi, spread_lo, taps,
         update, deformed, img, ypad, yf, ysend, yrecv, zmid, zrecv, zmid_edge, zrecv_edge,
           zf, beyond, zshift, yshift_send, yshift, rim, rim_rows, rim_f, forces, ghat, msend, mrecv, coarse, parts, arrived, mixed, tall,
           zsum, fhi, flo, ys_send, ys_recv, zs_send, zs_recv, rs_send, rs_recv, zh_send, zh_recv, yh_send, yh_recv, ms_send, ms_recv,
           cs_send, cs_recv, hs_send, hs_recv):
    depth, rows, width = template.shape
    steps = shifts.shape[0]
    cz = 3 * depth
    me_y, me_z = lax.axis_index("gy"), lax.axis_index("gz")

    def at_y(offset):
        return (lax.rem(me_y + (offset + ny), ny), me_z)

    def at_z(offset):
        return (me_y, lax.rem(me_z + (offset + nz), nz))

    def copy(src, dst, send, recv, device):
        return pltpu.make_async_remote_copy(
            src_ref=src, dst_ref=dst, send_sem=send, recv_sem=recv, device_id=device,
            device_id_type=MESH)

    def rolled(value, by, axis):
        return pltpu.roll(value, by % value.shape[axis], axis)

    chunks = depth * EDGE // 8
    per = depth // chunks

    def y_copies(step, chunk):
        part = pl.ds(chunk * 8, 8)
        return [copy(ysend.at[step, side, part], yrecv.at[step, side, part],
                     ys_send.at[step, side, chunk], ys_recv.at[step, side, chunk],
                     at_y(1 - 2 * side)) for side in range(2)]

    inner = (((EDGE, rows - 2 * EDGE, 0),), zmid, zrecv, 0)
    outer = (((0, EDGE, 0), (rows - EDGE, EDGE, EDGE)), zmid_edge, zrecv_edge, 1)

    def z_copies(step, part, halo=HALO, side=None):
        _, mid, received, which = part
        if side is None:
            return [z_copies(step, part, halo, side) for side in range(2)]
        return copy(mid.at[step, pl.ds((1 - side) * (depth - halo), halo)],
                    received.at[step, side, pl.ds(0, halo)], zs_send.at[step, side, which],
                    zs_recv.at[step, side, which], at_z(1 - 2 * side))

    far_side = jnp.where(me_z < nz // 2, 1, 0)

    def start_z(step, part, halo=HALO):
        for side in (far_side, 1 - far_side):
            z_copies(step, part, halo, side).start()

    mine = pl.ds(2 * depth, 2 * depth)

    def rim_copies():
        return [copy(rim.at[mine], rim.at[pl.ds(side * 4 * depth, 2 * depth)],
                     rs_send.at[side], rs_recv.at[side], at_z(1 - 2 * side)) for side in range(2)]

    ahead = [copy(all_shifts.at[steps - 1, 2, depth - 1], zshift.at[0], zh_send.at[0],
                  zh_recv.at[0], at_z(1)),
             copy(all_shifts.at[steps - 1, 2, 0], zshift.at[1], zh_send.at[1], zh_recv.at[1],
                  at_z(-1)),
             copy(yshift_send.at[0], yshift.at[0], yh_send.at[0], yh_recv.at[0], at_y(1)),
             copy(yshift_send.at[1], yshift.at[1], yh_send.at[1], yh_recv.at[1], at_y(-1))]

    def take_edges(step, z):
        ypad[z, pl.ds(8 - EDGE, EDGE), :] = yrecv[step, 0, pl.ds(z * EDGE, EDGE), :]
        ypad[z, pl.ds(8 + rows, EDGE), :] = yrecv[step, 1, pl.ds(z * EDGE, EDGE), :]

    def pass_x(w, u, shift):
        f = (w[0] * rolled(u, 1, 1) + w[1] * u + w[2] * rolled(u, -1, 1)
             + w[3] * rolled(u, -2, 1))
        return choose(shift, (rolled(f, 2, 1), rolled(f, 1, 1), f, rolled(f, -1, 1)))

    def edges(step, source, start):
        w = cubic_weights(fractions[step, 0])
        first, last = pl.ds(0, EDGE), pl.ds(rows - EDGE, EDGE)
        for z in range(depth):
            value = pass_x(
                w, jnp.concatenate([source[z, first, :], source[z, last, :]], axis=0),
                jnp.concatenate([shifts[step, 0, z, first, :], shifts[step, 0, z, last, :]],
                                axis=0))
            ypad[z, pl.ds(8, EDGE), :] = value[:EDGE, :]
            ypad[z, pl.ds(8 + rows - EDGE, EDGE), :] = value[EDGE:, :]
            ysend[step, 0, pl.ds(z * EDGE, EDGE), :] = value[EDGE:, :]
            ysend[step, 1, pl.ds(z * EDGE, EDGE), :] = value[:EDGE, :]
            if start and z % per == per - 1:
                for c in y_copies(step, z // per):
                    c.start()

    def rest(step, source, last):
        halo = HALO + 1 if last else HALO
        w_x = cubic_weights(fractions[step, 0])
        middle = pl.ds(EDGE, rows - 2 * EDGE)
        for z in range(depth):
            ypad[z, pl.ds(8 + EDGE, rows - 2 * EDGE), :] = pass_x(
                w_x, source[z, middle, :], shifts[step, 0, z, middle, :])
        w = cubic_weights(fractions[step, 1])

        def pass_y(part, z):
            for start, count, at in part[0]:
                f = w[0] * ypad[z, pl.ds(5 + start, count + 3), :]
                for n in range(1, 4):
                    f = f + w[n] * ypad[z, pl.ds(5 + start + n, count + 3), :]
                yf[z, pl.ds(0, count + 3), :] = f
                part[1][step, z, pl.ds(at, count), :] = choose(
                    shifts[step, 1, z, pl.ds(start, count), :],
                    [yf[z, pl.ds(o, count), :] for o in range(4)])

        for z in range(depth):
            pass_y(inner, z)
        start_z(step, inner, halo)
        for z in range(depth):
            if z % per == 0:
                for c in y_copies(step, z // per):
                    c.wait_recv()
            take_edges(step, z)
            if last:
                for m in range(7):
                    rim_rows[m, pl.ds(2 * z, 1), :] = ypad[z, pl.ds(4 + m, 1), :]
                    rim_rows[m, pl.ds(2 * z + 1, 1), :] = ypad[z, pl.ds(5 + rows + m, 1), :]
            pass_y(outer, z)
        if last:
            for c in ahead:
                c.wait_recv()
            odd = lax.broadcasted_iota(jnp.int32, (2 * depth, width), 0) % 2 == 1

            def rim_shift(at):
                part = pl.ds(at, 2 * depth)
                return jnp.where(odd, yshift[1, part, :], yshift[0, part, :])

            rim[mine, :] = choose(rim_shift(2 * depth), [
                w[0] * rim_rows[o] + w[1] * rim_rows[o + 1] + w[2] * rim_rows[o + 2]
                + w[3] * rim_rows[o + 3] for o in range(4)])
            for c in rim_copies():
                c.start()
        start_z(step, outer, halo)
        w_z = cubic_weights(fractions[step, 2])

        def pass_z(part):
            pieces, mid, received, _ = part
            for c in z_copies(step, part, halo):
                c.wait_recv()
            size = sum(count for _, count, _ in pieces)

            def layer(k):
                if k < 0:
                    return received[step, 0, halo + k]
                if k < depth:
                    return mid[step, k]
                return received[step, 1, k - depth]

            low = 1 - halo
            for k in range(low, depth + halo - 2):
                zf[k - low, pl.ds(0, size), :] = (w_z[0] * layer(k - 1) + w_z[1] * layer(k)
                                                  + w_z[2] * layer(k + 1) + w_z[3] * layer(k + 2))
            for z in range(-1, depth + 1) if last else range(depth):
                for start, count, at in pieces:
                    part = pl.ds(start, count)
                    options = [zf[z + o - 2 - low, pl.ds(at, count), :] for o in range(4)]
                    if z < 0:
                        beyond[0, part, :] = choose(zshift[0, part, :], options)
                    elif z == depth:
                        beyond[1, part, :] = choose(zshift[1, part, :], options)
                    else:
                        img[z, part, :] = choose(shifts[step, 2, z, part, :], options)

        pass_z(inner)
        if last:
            for c in rim_copies():
                c.wait_recv()
            span = 2 * (depth + 3)
            f = w_z[0] * rim[pl.ds(2 * depth - 6, span), :]
            for n in range(1, 4):
                f = f + w_z[n] * rim[pl.ds(2 * depth - 6 + 2 * n, span), :]
            rim_f[...] = f
            value = choose(rim_shift(0), [rim_f[pl.ds(2 * o, 2 * depth), :] for o in range(4)])
            for z in range(depth):
                ypad[z, pl.ds(7, 1), :] = value[2 * z:2 * z + 1, :]
                ypad[z, pl.ds(8 + rows, 1), :] = value[2 * z + 1:2 * z + 2, :]
        pass_z(outer)
        for chunk in range(chunks):
            for c in y_copies(step, chunk):
                c.wait_send()
        for part in (inner, outer):
            for c in z_copies(step, part, halo):
                c.wait_send()
        if last:
            for c in ahead + rim_copies():
                c.wait_send()

    def advance(step, carry):
        rest(step, img, False)
        edges(step + 1, img, True)
        return carry

    fetches[12].wait()
    fetches[0].wait()
    fetch_shifts(0).wait()
    edges(0, template, False)
    for z in range(depth):
        img[z] = template[z]
    for step in range(1, steps):
        fetch_shifts(step).wait()
    for place, kind in enumerate((2, 1)):
        for z in range(depth):
            for side, row in enumerate((rows - 1, 0)):
                value = shifts[steps - 1, kind, z, pl.ds(row, 1), :]
                for twin in range(2):
                    yshift_send[side, pl.ds(2 * (place * depth + z) + twin, 1), :] = value
    mixed[...] = jnp.zeros_like(mixed)
    pl.semaphore_wait(pltpu.get_barrier_semaphore(), ny + nz - 2)
    for chunk in range(chunks):
        for c in y_copies(0, chunk):
            c.start()
    for c in ahead:
        c.start()
    lax.fori_loop(0, steps - 1, advance, 0)
    rest(steps - 1, img, True)

    fetches[1].wait()
    for z in range(depth):
        u = img[z]
        deformed[z] = u
        ypad[z, pl.ds(8, rows), :] = u
        mismatch = u - target[z]
        forces[pl.ds(z * rows, rows), :] = (
            mismatch * ((rolled(u, -1, 1) - rolled(u, 1, 1)) * 0.5))
        grad = (ypad[z, pl.ds(9, rows), :] - ypad[z, pl.ds(7, rows), :]) * 0.5
        forces[pl.ds((depth + z) * rows, rows), :] = mismatch * grad
        above = img[z + 1] if z + 1 < depth else beyond[1]
        below = img[z - 1] if z > 0 else beyond[0]
        forces[pl.ds((2 * depth + z) * rows, rows), :] = mismatch * ((above - below) * 0.5)

    dc, rc, wc = depth // 2, rows // 2, width // 2
    lanes = min(wc, 128)
    for c in range(3):
        for z in range(dc):
            base = (c * depth + 2 * z) * rows
            zsum[pl.ds((c * dc + z) * rows, rows), :] = (
                forces[pl.ds(base, rows), :] + forces[pl.ds(base + rows, rows), :])
    for i in (7, 8):
        fetches[i].wait()
    high, low = split(zsum[...])
    folded = dot3(high, low, fold_hi[...], fold_lo[...])
    pairs = 3 * dc * rc
    for h in range(wc // lanes):
        across = pl.ds(h * lanes, lanes)
        tall[h] = folded[:, h * lanes:(h + 1) * lanes]
        coarse[0, :, across] = (tall[h, pl.ds(0, pairs, stride=2), :]
                                + tall[h, pl.ds(1, pairs, stride=2), :])
    per_c = dc * rc

    def gather(d, c, device):
        return copy(coarse.at[0, pl.ds(c * per_c, per_c)], coarse.at[d, pl.ds(c * per_c, per_c)],
                    cs_send.at[d - 1, c], cs_recv.at[d - 1, c], device)

    for k in range(nz - 1):
        away = jnp.where(me_z < nz // 2, nz - 1 - k, k)
        away = away + jnp.where(me_z < nz // 2, -(away <= me_z).astype(jnp.int32),
                                (away >= me_z).astype(jnp.int32))
        for c in range(3):
            gather(lax.rem(me_z - away + nz, nz), c, (me_y, away)).start()

    for i in (3, 4, 5):
        fetches[i].wait()
    high, low = split(forces[...])
    ghat[...] = dot3(high, low, hart_hi[...], hart_lo[...])
    for k in range(cz):
        g = ghat[pl.ds(k * rows, rows), :]
        msend[pl.ds(k, 1), :] = jnp.sum(g * tables[0], axis=0, keepdims=True)
        msend[pl.ds(cz + k, 1), :] = jnp.sum(g * tables[1], axis=0, keepdims=True)
    odd_core = lax.rem(me_y, 2)
    partner = (me_y + 1 - 2 * odd_core, me_z)

    def moment(d):
        return copy(msend, mrecv.at[d - 1], ms_send.at[d - 1], ms_recv.at[d - 1], at_y(d))

    def to_partner(d):
        slot = lax.rem(d + ny - 2 * odd_core, ny)
        return copy(msend if d == 0 else mrecv.at[d - 1], mrecv.at[slot], ms_send.at[d],
                    ms_recv.at[slot], partner)

    for d in range(2, ny, 2):
        moment(d).start()
    to_partner(0).start()
    levels = (tables.shape[0] - 5) // 2
    for k in range(cz):
        g = ghat[pl.ds(k * rows, rows), :]
        down, up = g, g
        for level in range(levels):
            down = down + tables[5 + level] * rolled(down, 1 << level, 0)
            up = up + tables[5 + levels + level] * rolled(up, -(1 << level), 0)
        ghat[pl.ds(k * rows, rows), :] = tables[4] * (down + (up - g))
    fetches[11].wait()
    sides = [[copy(parts.at[1 + side, pl.ds(c * dc * rc, dc * rc)],
                   arrived.at[side, pl.ds(c * dc * rc, dc * rc)], hs_send.at[side, c],
                   hs_recv.at[side, c], at_y(2 * side - 1)) for side in range(2)]
             for c in range(3)]
    total, far = nz * dc, far_layers(nz * dc)
    for c in range(3):
        for d in range(1, nz):
            gather(d, c, at_z(-d)).wait()
        for h in range(wc // lanes):
            across = pl.ds(h * lanes, lanes)

            def level(z, c=c, across=across):
                return coarse[z % total // dc, pl.ds((c * dc + z % dc) * rc, rc), across]

            for a in range(dc):
                for dz in range(far):
                    value = level(a + dz)
                    if 0 < dz and 2 * dz != total:
                        value = value + level(a + total - dz)
                    mixed[h, a * far + dz, pl.ds(rc, rc), :] = value
            for a in range(dc):
                sums = [None] * 3

                def add(side, value):
                    sums[side] = value if sums[side] is None else sums[side] + value

                row = 0
                for dz in range(far):
                    for dy in range(CHEB - dz):
                        tap = taps[pl.ds(row, 1), across]
                        row += 1
                        at = [mixed[h, a * far + dz, pl.ds(o, rc), :]
                              for o in (dy, rc - dy, rc + dy, 2 * rc - dy)]
                        if dy == 0:
                            add(0, tap * at[1])
                        else:
                            add(0, tap * (at[1] + at[2]))
                            add(1, tap * at[0])
                            add(2, tap * at[3])
                for side in range(3):
                    parts[side, pl.ds((c * dc + a) * rc, rc), across] = sums[side]
        for side in sides[c]:
            side.start()
        if c == 0:
            for d in range(2, ny, 2):
                moment(d).wait_recv()
                to_partner(d).start()
    for d in range(1, ny, 2):
        moment(d).wait_recv()
    for d in range(2, ny, 2):
        moment(d).wait_send()
    for d in range(0, ny, 2):
        to_partner(d).wait_send()
    fetches[6].wait()
    from_left = hops[pl.ds(ny - 1, 1), :] * msend[pl.ds(0, cz), :]
    from_right = hops[pl.ds(ny - 1, 1), :] * msend[pl.ds(cz, cz), :]
    for m in range(1, ny):
        from_left = from_left + hops[pl.ds(m - 1, 1), :] * mrecv[m - 1, pl.ds(0, cz), :]
        from_right = from_right + hops[pl.ds(m - 1, 1), :] * mrecv[ny - m - 1, pl.ds(cz, cz), :]
    for k in range(cz):
        s = (ghat[pl.ds(k * rows, rows), :] + tables[2] * from_left[k:k + 1, :]
             + tables[3] * from_right[k:k + 1, :])
        high, low = split(s)
        fhi[pl.ds(k * rows, rows), :] = high
        flo[pl.ds(k * rows, rows), :] = low
    ghat[...] = dot3(fhi[...], flo[...], hart_hi[...], hart_lo[...])

    for i in (9, 10):
        fetches[i].wait()
    for pair in sides:
        for c in pair:
            c.wait()
    high, low = split(parts[0] + (arrived[0] + arrived[1]))
    short = dot3(high, low, spread_hi[...], spread_lo[...])
    for h in range(width // lanes):
        value = short[:, h * lanes:(h + 1) * lanes]
        for twin in range(2):
            tall[h, pl.ds(twin, pairs, stride=2), :] = value
    for c in range(3):
        for z in range(depth):
            for h in range(width // lanes):
                across = pl.ds(h * lanes, lanes)
                fine = tall[h, pl.ds((c * dc + z // 2) * rows, rows), :]
                update[c, z, :, across] = -(ghat[pl.ds((c * depth + z) * rows, rows), across]
                                            + fine)


def on_device(template, target, shifts, fractions, *, ny, nz):
    depth, rows, width = template.shape
    steps = shifts.shape[0]
    dc, rc, wc = depth // 2, rows // 2, width // 2
    cz = 3 * depth
    hart_hi, hart_lo, tables, hops = make_tables(rows, width, ny)
    fold_hi, fold_lo, spread_hi, spread_lo, taps = make_coarse(width, nz * dc, ny * rc)
    f32, bf16 = jnp.float32, jnp.bfloat16
    vmem, dma = pltpu.VMEM, pltpu.SemaphoreType.DMA
    scratch = [
        vmem((depth, rows, width), f32),
        vmem((depth, rows + 16, width), f32),
        vmem((depth, rows + 8, width), f32),
        vmem((steps, 2, depth * EDGE, width), f32),
        vmem((steps, 2, depth * EDGE, width), f32),
        vmem((steps, depth, rows - 2 * EDGE, width), f32),
        vmem((steps, 2, HALO + 1, rows - 2 * EDGE, width), f32),
        vmem((steps, depth, 2 * EDGE, width), f32),
        vmem((steps, 2, HALO + 1, 2 * EDGE, width), f32),
        vmem((depth + 5, rows, width), f32),
        vmem((2, rows, width), f32),
        vmem((2, rows, width), shifts.dtype),
        vmem((2, 4 * depth, width), shifts.dtype),
        vmem((2, 4 * depth, width), shifts.dtype),
        vmem((6 * depth, width), f32),
        vmem((7, 2 * depth, width), f32),
        vmem((2 * (depth + 3), width), f32),
        vmem((cz * rows, width), f32),
        vmem((cz * rows, width), f32),
        vmem((2 * cz, width), f32),
        vmem((ny - 1, 2 * cz, width), f32),
        vmem((nz, 3 * dc * rc, wc), f32),
        vmem((3, 3 * dc * rc, wc), f32),
        vmem((2, 3 * dc * rc, wc), f32),
        vmem((-(-wc // 128), dc * far_layers(nz * dc), 3 * rc, min(wc, 128)), f32),
        vmem((width // min(wc, 128), 3 * dc * rows, min(wc, 128)), f32),
        vmem((3 * dc * rows, width), f32),
        vmem((cz * rows, width), bf16),
        vmem((cz * rows, width), bf16),
        dma((steps, 2, depth * EDGE // 8)), dma((steps, 2, depth * EDGE // 8)),
        dma((steps, 2, 2)), dma((steps, 2, 2)),
        dma((2,)), dma((2,)), dma((2,)), dma((2,)), dma((2,)), dma((2,)),
        dma((ny - 1,)), dma((ny - 1,)),
        dma((nz - 1, 3)), dma((nz - 1, 3)),
        dma((2, 3)), dma((2, 3)),
    ]
    spec = pl.BlockSpec(memory_space=pltpu.VMEM)
    hbm = pl.BlockSpec(memory_space=pltpu.HBM)
    operands = [template, target, shifts, jnp.asarray(hart_hi), jnp.asarray(hart_lo),
                *map(jnp.asarray, (tables, hops, fold_hi, fold_lo, spread_hi, spread_lo, taps)),
                fractions]
    held = [vmem(x.shape, x.dtype) for x in operands[:-1]] + [pltpu.SMEM(fractions.shape, f32)]
    scratch = held + [dma((len(operands),)), dma((steps,))] + scratch
    return tuple(pl.pallas_call(
        functools.partial(kernel, ny, nz),
        out_shape=(vmem((3, depth, rows, width), f32), vmem((depth, rows, width), f32)),
        in_specs=[hbm] * len(operands),
        out_specs=(spec, spec),
        scratch_shapes=scratch,
        compiler_params=pltpu.CompilerParams(
            collective_id=0, has_side_effects=True),
    )(*operands))


def solution(mesh):
    return jax.shard_map(
        functools.partial(on_device, ny=mesh.shape["gy"], nz=mesh.shape["gz"]),
        mesh=mesh,
        in_specs=(P("gz", "gy", None), P("gz", "gy", None), P(None, None, "gz", "gy", None), P()),
        out_specs=(P(None, "gz", "gy", None), P("gz", "gy", None)),
        check_vma=False,
    )
```

```python
import functools

import jax
import jax.numpy as jnp
import numpy as np
from jax import lax
from jax.experimental import pallas as pl
from jax.experimental.pallas import tpu as pltpu
from jax.sharding import PartitionSpec as P

CHEB = 8
DAMPING = 0.25
ACROSS_WEIGHT = 0.0625
ALONG_SCALE = 32.0
SHIFT = 0.25
MESH = pl.DeviceIdType.MESH
EDGE = 4
HALO = 3


def cubic_weights(fraction):
    return (
        -fraction * (fraction - 1.0) * (fraction - 2.0) / 6.0,
        (fraction + 1.0) * (fraction - 1.0) * (fraction - 2.0) / 2.0,
        -(fraction + 1.0) * fraction * (fraction - 2.0) / 2.0,
        (fraction + 1.0) * fraction * (fraction - 1.0) / 6.0,
    )


def turn_factors(count):
    low, high = SHIFT, SHIFT + 12.0
    theta, delta = (high + low) / 2.0, (high - low) / 2.0
    sigma = theta / delta
    now = 1.0 / sigma
    factors = []
    for _ in range(count - 1):
        after = 1.0 / (2.0 * sigma - now)
        factors.append((after * now, 2.0 * after / delta))
        now = after
    return theta, factors


def make_tables(rows, length_x, peers):
    length_y = rows * peers
    index = np.arange(length_x)
    angle = 2.0 * np.pi / length_x * (np.outer(index, index) % length_x)
    hartley = np.cos(angle) + np.sin(angle)
    weight = (length_y / ALONG_SCALE) ** 2
    a = DAMPING + 4.0 * ACROSS_WEIGHT * np.sin(np.pi * index / length_x) ** 2
    half = a / (2.0 * weight)
    r = 1.0 / (1.0 + half + np.sqrt(half * (half + 2.0)))
    y = np.arange(rows)[:, None]
    scale = 1.0 / (weight * (1.0 / r - r) * length_x)
    down, up, stride = [], [], 1
    while stride < rows:
        down.append(np.where(y >= stride, r ** stride, 0.0))
        up.append(np.where(y < rows - stride, r ** stride, 0.0))
        stride *= 2
    tables = [r ** (rows - 1 - y), r ** y, scale * r ** (y + 1), scale * r ** (rows - y),
              scale + 0.0 * r * y] + down + up
    m = np.arange(peers)[:, None]
    hops = r ** (rows * m) / (1.0 - r ** length_y)
    high = hartley.astype(jnp.bfloat16)
    low = (hartley - high.astype(np.float64)).astype(jnp.bfloat16)
    return high, low, np.stack(tables).astype(np.float32), hops.astype(np.float32)


def cas(length):
    index = np.arange(length)
    angle = 2.0 * np.pi / length * (np.outer(index, index) % length)
    return np.cos(angle) + np.sin(angle)


def in_two(table):
    high = table.astype(jnp.bfloat16)
    return high, (table - high.astype(np.float64)).astype(jnp.bfloat16)


def far_layers(total):
    return min(total // 2, CHEB - 1) + 1


def make_coarse(width, total, length_y):
    half = width // 2
    pair = np.kron(np.eye(half), np.full((2, 1), 0.125))
    fold = in_two(pair @ cas(half))
    spread = in_two(cas(half) @ np.kron(np.eye(half), np.ones((1, 2))) / half)
    x, y, z = [2.0 * np.cos(2.0 * np.pi * np.arange(n) / n) for n in (half, length_y, total)]
    symbol = SHIFT + 6.0 - (z[:, None, None] + y[None, :, None] + x[None, None, :])
    theta, factors = turn_factors(CHEB)
    residual = np.ones_like(symbol)
    direction = residual / theta
    gain = direction
    for keep, add in factors:
        residual = residual - symbol * direction
        direction = keep * direction + add * residual
        gain = gain + direction
    taps = []
    for dz in range(far_layers(total)):
        in_z = np.cos(2.0 * np.pi * dz * np.arange(total) / total) / total
        plane = np.tensordot(in_z, gain, 1)
        for dy in range(CHEB - dz):
            in_y = np.cos(2.0 * np.pi * dy * np.arange(length_y) / length_y) / length_y
            taps.append(in_y @ plane)
    return fold + spread + (np.stack(taps).astype(np.float32),)


def dot3(high, low, table_high, table_low):
    f = functools.partial(jnp.dot, preferred_element_type=jnp.float32)
    return f(high, table_high) + (f(low, table_high) + f(high, table_low))


def split(value):
    high = value.astype(jnp.bfloat16)
    return high, (value - high.astype(jnp.float32)).astype(jnp.bfloat16)


def choose(shift, options):
    minus2, minus1, zero, one = options
    result = jnp.where(shift == 0, zero, one)
    result = jnp.where(shift == -1, minus1, result)
    return jnp.where(shift == -2, minus2, result)


def kernel(ny, nz, *refs):
    me_y, me_z = lax.axis_index("gy"), lax.axis_index("gz")
    barrier = pltpu.get_barrier_semaphore()
    for d in range(1, ny):
        pl.semaphore_signal(barrier, inc=1, device_id=(lax.rem(me_y + d, ny), me_z),
                            device_id_type=MESH)
    for d in range(1, nz):
        pl.semaphore_signal(barrier, inc=1, device_id=(me_y, lax.rem(me_z + d, nz)),
                            device_id_type=MESH)
    count = 13
    sources, (update, deformed), rest = refs[:count], refs[count:count + 2], refs[count + 2:]
    held, fetch_sems, shift_sems = rest[:count], rest[count], rest[count + 1]
    step_count = held[2].shape[0]
    fetches = {}
    for i in (0, 1, *range(3, count)):
        fetches[i] = pltpu.make_async_copy(sources[i], held[i], fetch_sems.at[i])

    def fetch_shifts(step):
        return pltpu.make_async_copy(sources[2].at[step], held[2].at[step], shift_sems.at[step])

    fetches[0].start()
    fetches[12].start()
    for step in range(step_count):
        fetch_shifts(step).start()
    for i in (1, 7, 8, 3, 4, 5, 6, 11, 9, 10):
        fetches[i].start()
    body(ny, nz, held[12], fetches, fetch_shifts, sources[2], *held[:12], update, deformed, *rest[count + 2:])


def body(ny, nz, fractions, fetches, fetch_shifts, all_shifts, template, target, shifts, hart_hi, hart_lo,
         tables, hops, fold_hi, fold_lo, spread_hi, spread_lo, taps,
         update, deformed, img, ypad, yf, ysend, yrecv, zmid, zrecv, zmid_edge, zrecv_edge,
           zf, beyond, zshift, yshift_send, yshift, rim, rim_rows, rim_f, forces, ghat, msend, mrecv, coarse, parts, arrived, mixed, tall,
           zsum, fhi, flo, ys_send, ys_recv, zs_send, zs_recv, rs_send, rs_recv, zh_send, zh_recv, yh_send, yh_recv, ms_send, ms_recv,
           cs_send, cs_recv, hs_send, hs_recv):
    depth, rows, width = template.shape
    steps = shifts.shape[0]
    cz = 3 * depth
    me_y, me_z = lax.axis_index("gy"), lax.axis_index("gz")

    def at_y(offset):
        return (lax.rem(me_y + (offset + ny), ny), me_z)

    def at_z(offset):
        return (me_y, lax.rem(me_z + (offset + nz), nz))

    def copy(src, dst, send, recv, device):
        return pltpu.make_async_remote_copy(
            src_ref=src, dst_ref=dst, send_sem=send, recv_sem=recv, device_id=device,
            device_id_type=MESH)

    def rolled(value, by, axis):
        return pltpu.roll(value, by % value.shape[axis], axis)

    chunks = depth * EDGE // 8
    per = depth // chunks

    def y_copies(step, chunk):
        part = pl.ds(chunk * 8, 8)
        return [copy(ysend.at[step, side, part], yrecv.at[step, side, part],
                     ys_send.at[step, side, chunk], ys_recv.at[step, side, chunk],
                     at_y(1 - 2 * side)) for side in range(2)]

    inner = (((EDGE, rows - 2 * EDGE, 0),), zmid, zrecv, 0)
    outer = (((0, EDGE, 0), (rows - EDGE, EDGE, EDGE)), zmid_edge, zrecv_edge, 1)

    def z_copies(step, part, halo=HALO, side=None):
        _, mid, received, which = part
        if side is None:
            return [z_copies(step, part, halo, side) for side in range(2)]
        return copy(mid.at[step, pl.ds((1 - side) * (depth - halo), halo)],
                    received.at[step, side, pl.ds(0, halo)], zs_send.at[step, side, which],
                    zs_recv.at[step, side, which], at_z(1 - 2 * side))

    far_side = jnp.where(me_z < nz // 2, 1, 0)

    def start_z(step, part, halo=HALO):
        for side in (far_side, 1 - far_side):
            z_copies(step, part, halo, side).start()

    mine = pl.ds(2 * depth, 2 * depth)

    def rim_copies():
        return [copy(rim.at[mine], rim.at[pl.ds(side * 4 * depth, 2 * depth)],
                     rs_send.at[side], rs_recv.at[side], at_z(1 - 2 * side)) for side in range(2)]

    ahead = [copy(all_shifts.at[steps - 1, 2, depth - 1], zshift.at[0], zh_send.at[0],
                  zh_recv.at[0], at_z(1)),
             copy(all_shifts.at[steps - 1, 2, 0], zshift.at[1], zh_send.at[1], zh_recv.at[1],
                  at_z(-1)),
             copy(yshift_send.at[0], yshift.at[0], yh_send.at[0], yh_recv.at[0], at_y(1)),
             copy(yshift_send.at[1], yshift.at[1], yh_send.at[1], yh_recv.at[1], at_y(-1))]

    def take_edges(step, z):
        ypad[z, pl.ds(8 - EDGE, EDGE), :] = yrecv[step, 0, pl.ds(z * EDGE, EDGE), :]
        ypad[z, pl.ds(8 + rows, EDGE), :] = yrecv[step, 1, pl.ds(z * EDGE, EDGE), :]

    def pass_x(w, u, shift):
        at = [rolled(u, 3 - m, 1) if m != 3 else u for m in range(7)]
        picked = [choose(shift, at[n:n + 4]) for n in range(4)]
        return w[0] * picked[0] + w[1] * picked[1] + w[2] * picked[2] + w[3] * picked[3]

    def edges(step, source, start):
        w = cubic_weights(fractions[step, 0])
        first, last = pl.ds(0, EDGE), pl.ds(rows - EDGE, EDGE)
        for z in range(depth):
            value = pass_x(
                w, jnp.concatenate([source[z, first, :], source[z, last, :]], axis=0),
                jnp.concatenate([shifts[step, 0, z, first, :], shifts[step, 0, z, last, :]],
                                axis=0))
            ypad[z, pl.ds(8, EDGE), :] = value[:EDGE, :]
            ypad[z, pl.ds(8 + rows - EDGE, EDGE), :] = value[EDGE:, :]
            ysend[step, 0, pl.ds(z * EDGE, EDGE), :] = value[EDGE:, :]
            ysend[step, 1, pl.ds(z * EDGE, EDGE), :] = value[:EDGE, :]
            if start and z % per == per - 1:
                for c in y_copies(step, z // per):
                    c.start()

    def rest(step, source, last):
        halo = HALO + 1 if last else HALO
        w_x = cubic_weights(fractions[step, 0])
        middle = pl.ds(EDGE, rows - 2 * EDGE)
        for z in range(depth):
            ypad[z, pl.ds(8 + EDGE, rows - 2 * EDGE), :] = pass_x(
                w_x, source[z, middle, :], shifts[step, 0, z, middle, :])
        w = cubic_weights(fractions[step, 1])

        def pass_y(part, z):
            for start, count, at in part[0]:
                f = w[0] * ypad[z, pl.ds(5 + start, count + 3), :]
                for n in range(1, 4):
                    f = f + w[n] * ypad[z, pl.ds(5 + start + n, count + 3), :]
                yf[z, pl.ds(0, count + 3), :] = f
                part[1][step, z, pl.ds(at, count), :] = choose(
                    shifts[step, 1, z, pl.ds(start, count), :],
                    [yf[z, pl.ds(o, count), :] for o in range(4)])

        for z in range(depth):
            pass_y(inner, z)
        start_z(step, inner, halo)
        for z in range(depth):
            if z % per == 0:
                for c in y_copies(step, z // per):
                    c.wait_recv()
            take_edges(step, z)
            if last:
                for m in range(7):
                    rim_rows[m, pl.ds(2 * z, 1), :] = ypad[z, pl.ds(4 + m, 1), :]
                    rim_rows[m, pl.ds(2 * z + 1, 1), :] = ypad[z, pl.ds(5 + rows + m, 1), :]
            pass_y(outer, z)
        if last:
            for c in ahead:
                c.wait_recv()
            odd = lax.broadcasted_iota(jnp.int32, (2 * depth, width), 0) % 2 == 1

            def rim_shift(at):
                part = pl.ds(at, 2 * depth)
                return jnp.where(odd, yshift[1, part, :], yshift[0, part, :])

            rim[mine, :] = choose(rim_shift(2 * depth), [
                w[0] * rim_rows[o] + w[1] * rim_rows[o + 1] + w[2] * rim_rows[o + 2]
                + w[3] * rim_rows[o + 3] for o in range(4)])
            for c in rim_copies():
                c.start()
        start_z(step, outer, halo)
        w_z = cubic_weights(fractions[step, 2])

        def pass_z(part):
            pieces, mid, received, _ = part
            for c in z_copies(step, part, halo):
                c.wait_recv()
            size = sum(count for _, count, _ in pieces)

            def layer(k):
                if k < 0:
                    return received[step, 0, halo + k]
                if k < depth:
                    return mid[step, k]
                return received[step, 1, k - depth]

            low = 1 - halo
            for k in range(low, depth + halo - 2):
                zf[k - low, pl.ds(0, size), :] = (w_z[0] * layer(k - 1) + w_z[1] * layer(k)
                                                  + w_z[2] * layer(k + 1) + w_z[3] * layer(k + 2))
            for z in range(-1, depth + 1) if last else range(depth):
                for start, count, at in pieces:
                    part = pl.ds(start, count)
                    options = [zf[z + o - 2 - low, pl.ds(at, count), :] for o in range(4)]
                    if z < 0:
                        beyond[0, part, :] = choose(zshift[0, part, :], options)
                    elif z == depth:
                        beyond[1, part, :] = choose(zshift[1, part, :], options)
                    else:
                        img[z, part, :] = choose(shifts[step, 2, z, part, :], options)

        pass_z(inner)
        if last:
            for c in rim_copies():
                c.wait_recv()
            span = 2 * (depth + 3)
            f = w_z[0] * rim[pl.ds(2 * depth - 6, span), :]
            for n in range(1, 4):
                f = f + w_z[n] * rim[pl.ds(2 * depth - 6 + 2 * n, span), :]
            rim_f[...] = f
            value = choose(rim_shift(0), [rim_f[pl.ds(2 * o, 2 * depth), :] for o in range(4)])
            for z in range(depth):
                ypad[z, pl.ds(7, 1), :] = value[2 * z:2 * z + 1, :]
                ypad[z, pl.ds(8 + rows, 1), :] = value[2 * z + 1:2 * z + 2, :]
        pass_z(outer)
        for chunk in range(chunks):
            for c in y_copies(step, chunk):
                c.wait_send()
        for part in (inner, outer):
            for c in z_copies(step, part, halo):
                c.wait_send()
        if last:
            for c in ahead + rim_copies():
                c.wait_send()

    def advance(step, carry):
        rest(step, img, False)
        edges(step + 1, img, True)
        return carry

    fetches[12].wait()
    fetches[0].wait()
    fetch_shifts(0).wait()
    edges(0, template, False)
    for z in range(depth):
        img[z] = template[z]
    for step in range(1, steps):
        fetch_shifts(step).wait()
    for place, kind in enumerate((2, 1)):
        for z in range(depth):
            for side, row in enumerate((rows - 1, 0)):
                value = shifts[steps - 1, kind, z, pl.ds(row, 1), :]
                for twin in range(2):
                    yshift_send[side, pl.ds(2 * (place * depth + z) + twin, 1), :] = value
    mixed[...] = jnp.zeros_like(mixed)
    pl.semaphore_wait(pltpu.get_barrier_semaphore(), ny + nz - 2)
    for chunk in range(chunks):
        for c in y_copies(0, chunk):
            c.start()
    for c in ahead:
        c.start()
    lax.fori_loop(0, steps - 1, advance, 0)
    rest(steps - 1, img, True)

    fetches[1].wait()
    for z in range(depth):
        u = img[z]
        deformed[z] = u
        ypad[z, pl.ds(8, rows), :] = u
        mismatch = u - target[z]
        forces[pl.ds(z * rows, rows), :] = (
            mismatch * ((rolled(u, -1, 1) - rolled(u, 1, 1)) * 0.5))
        grad = (ypad[z, pl.ds(9, rows), :] - ypad[z, pl.ds(7, rows), :]) * 0.5
        forces[pl.ds((depth + z) * rows, rows), :] = mismatch * grad
        above = img[z + 1] if z + 1 < depth else beyond[1]
        below = img[z - 1] if z > 0 else beyond[0]
        forces[pl.ds((2 * depth + z) * rows, rows), :] = mismatch * ((above - below) * 0.5)

    dc, rc, wc = depth // 2, rows // 2, width // 2
    lanes = min(wc, 128)
    for c in range(3):
        for z in range(dc):
            base = (c * depth + 2 * z) * rows
            zsum[pl.ds((c * dc + z) * rows, rows), :] = (
                forces[pl.ds(base, rows), :] + forces[pl.ds(base + rows, rows), :])
    for i in (7, 8):
        fetches[i].wait()
    high, low = split(zsum[...])
    folded = dot3(high, low, fold_hi[...], fold_lo[...])
    pairs = 3 * dc * rc
    for h in range(wc // lanes):
        across = pl.ds(h * lanes, lanes)
        tall[h] = folded[:, h * lanes:(h + 1) * lanes]
        coarse[0, :, across] = (tall[h, pl.ds(0, pairs, stride=2), :]
                                + tall[h, pl.ds(1, pairs, stride=2), :])
    per_c = dc * rc

    def gather(d, c, device):
        return copy(coarse.at[0, pl.ds(c * per_c, per_c)], coarse.at[d, pl.ds(c * per_c, per_c)],
                    cs_send.at[d - 1, c], cs_recv.at[d - 1, c], device)

    for k in range(nz - 1):
        away = jnp.where(me_z < nz // 2, nz - 1 - k, k)
        away = away + jnp.where(me_z < nz // 2, -(away <= me_z).astype(jnp.int32),
                                (away >= me_z).astype(jnp.int32))
        for c in range(3):
            gather(lax.rem(me_z - away + nz, nz), c, (me_y, away)).start()

    for i in (3, 4, 5):
        fetches[i].wait()
    high, low = split(forces[...])
    ghat[...] = dot3(high, low, hart_hi[...], hart_lo[...])
    for k in range(cz):
        g = ghat[pl.ds(k * rows, rows), :]
        msend[pl.ds(k, 1), :] = jnp.sum(g * tables[0], axis=0, keepdims=True)
        msend[pl.ds(cz + k, 1), :] = jnp.sum(g * tables[1], axis=0, keepdims=True)
    odd_core = lax.rem(me_y, 2)
    partner = (me_y + 1 - 2 * odd_core, me_z)

    def moment(d):
        return copy(msend, mrecv.at[d - 1], ms_send.at[d - 1], ms_recv.at[d - 1], at_y(d))

    def to_partner(d):
        slot = lax.rem(d + ny - 2 * odd_core, ny)
        return copy(msend if d == 0 else mrecv.at[d - 1], mrecv.at[slot], ms_send.at[d],
                    ms_recv.at[slot], partner)

    for d in range(2, ny, 2):
        moment(d).start()
    to_partner(0).start()
    levels = (tables.shape[0] - 5) // 2
    for k in range(cz):
        g = ghat[pl.ds(k * rows, rows), :]
        down, up = g, g
        for level in range(levels):
            down = down + tables[5 + level] * rolled(down, 1 << level, 0)
            up = up + tables[5 + levels + level] * rolled(up, -(1 << level), 0)
        ghat[pl.ds(k * rows, rows), :] = tables[4] * (down + (up - g))
    fetches[11].wait()
    sides = [[copy(parts.at[1 + side, pl.ds(c * dc * rc, dc * rc)],
                   arrived.at[side, pl.ds(c * dc * rc, dc * rc)], hs_send.at[side, c],
                   hs_recv.at[side, c], at_y(2 * side - 1)) for side in range(2)]
             for c in range(3)]
    total, far = nz * dc, far_layers(nz * dc)
    for c in range(3):
        for d in range(1, nz):
            gather(d, c, at_z(-d)).wait()
        for h in range(wc // lanes):
            across = pl.ds(h * lanes, lanes)

            def level(z, c=c, across=across):
                return coarse[z % total // dc, pl.ds((c * dc + z % dc) * rc, rc), across]

            for a in range(dc):
                for dz in range(far):
                    value = level(a + dz)
                    if 0 < dz and 2 * dz != total:
                        value = value + level(a + total - dz)
                    mixed[h, a * far + dz, pl.ds(rc, rc), :] = value
            for a in range(dc):
                sums = [None] * 3

                def add(side, value):
                    sums[side] = value if sums[side] is None else sums[side] + value

                row = 0
                for dz in range(far):
                    for dy in range(CHEB - dz):
                        tap = taps[pl.ds(row, 1), across]
                        row += 1
                        at = [mixed[h, a * far + dz, pl.ds(o, rc), :]
                              for o in (dy, rc - dy, rc + dy, 2 * rc - dy)]
                        if dy == 0:
                            add(0, tap * at[1])
                        else:
                            add(0, tap * (at[1] + at[2]))
                            add(1, tap * at[0])
                            add(2, tap * at[3])
                for side in range(3):
                    parts[side, pl.ds((c * dc + a) * rc, rc), across] = sums[side]
        for side in sides[c]:
            side.start()
        if c == 0:
            for d in range(2, ny, 2):
                moment(d).wait_recv()
                to_partner(d).start()
    for d in range(1, ny, 2):
        moment(d).wait_recv()
    for d in range(2, ny, 2):
        moment(d).wait_send()
    for d in range(0, ny, 2):
        to_partner(d).wait_send()
    fetches[6].wait()
    from_left = hops[pl.ds(ny - 1, 1), :] * msend[pl.ds(0, cz), :]
    from_right = hops[pl.ds(ny - 1, 1), :] * msend[pl.ds(cz, cz), :]
    for m in range(1, ny):
        from_left = from_left + hops[pl.ds(m - 1, 1), :] * mrecv[m - 1, pl.ds(0, cz), :]
        from_right = from_right + hops[pl.ds(m - 1, 1), :] * mrecv[ny - m - 1, pl.ds(cz, cz), :]
    for k in range(cz):
        s = (ghat[pl.ds(k * rows, rows), :] + tables[2] * from_left[k:k + 1, :]
             + tables[3] * from_right[k:k + 1, :])
        high, low = split(s)
        fhi[pl.ds(k * rows, rows), :] = high
        flo[pl.ds(k * rows, rows), :] = low
    ghat[...] = dot3(fhi[...], flo[...], hart_hi[...], hart_lo[...])

    for i in (9, 10):
        fetches[i].wait()
    for pair in sides:
        for c in pair:
            c.wait()
    high, low = split(parts[0] + (arrived[0] + arrived[1]))
    short = dot3(high, low, spread_hi[...], spread_lo[...])
    for h in range(width // lanes):
        value = short[:, h * lanes:(h + 1) * lanes]
        for twin in range(2):
            tall[h, pl.ds(twin, pairs, stride=2), :] = value
    for c in range(3):
        for z in range(depth):
            for h in range(width // lanes):
                across = pl.ds(h * lanes, lanes)
                fine = tall[h, pl.ds((c * dc + z // 2) * rows, rows), :]
                update[c, z, :, across] = -(ghat[pl.ds((c * depth + z) * rows, rows), across]
                                            + fine)


def on_device(template, target, shifts, fractions, *, ny, nz):
    depth, rows, width = template.shape
    steps = shifts.shape[0]
    dc, rc, wc = depth // 2, rows // 2, width // 2
    cz = 3 * depth
    hart_hi, hart_lo, tables, hops = make_tables(rows, width, ny)
    fold_hi, fold_lo, spread_hi, spread_lo, taps = make_coarse(width, nz * dc, ny * rc)
    f32, bf16 = jnp.float32, jnp.bfloat16
    vmem, dma = pltpu.VMEM, pltpu.SemaphoreType.DMA
    scratch = [
        vmem((depth, rows, width), f32),
        vmem((depth, rows + 16, width), f32),
        vmem((depth, rows + 8, width), f32),
        vmem((steps, 2, depth * EDGE, width), f32),
        vmem((steps, 2, depth * EDGE, width), f32),
        vmem((steps, depth, rows - 2 * EDGE, width), f32),
        vmem((steps, 2, HALO + 1, rows - 2 * EDGE, width), f32),
        vmem((steps, depth, 2 * EDGE, width), f32),
        vmem((steps, 2, HALO + 1, 2 * EDGE, width), f32),
        vmem((depth + 5, rows, width), f32),
        vmem((2, rows, width), f32),
        vmem((2, rows, width), shifts.dtype),
        vmem((2, 4 * depth, width), shifts.dtype),
        vmem((2, 4 * depth, width), shifts.dtype),
        vmem((6 * depth, width), f32),
        vmem((7, 2 * depth, width), f32),
        vmem((2 * (depth + 3), width), f32),
        vmem((cz * rows, width), f32),
        vmem((cz * rows, width), f32),
        vmem((2 * cz, width), f32),
        vmem((ny - 1, 2 * cz, width), f32),
        vmem((nz, 3 * dc * rc, wc), f32),
        vmem((3, 3 * dc * rc, wc), f32),
        vmem((2, 3 * dc * rc, wc), f32),
        vmem((-(-wc // 128), dc * far_layers(nz * dc), 3 * rc, min(wc, 128)), f32),
        vmem((width // min(wc, 128), 3 * dc * rows, min(wc, 128)), f32),
        vmem((3 * dc * rows, width), f32),
        vmem((cz * rows, width), bf16),
        vmem((cz * rows, width), bf16),
        dma((steps, 2, depth * EDGE // 8)), dma((steps, 2, depth * EDGE // 8)),
        dma((steps, 2, 2)), dma((steps, 2, 2)),
        dma((2,)), dma((2,)), dma((2,)), dma((2,)), dma((2,)), dma((2,)),
        dma((ny - 1,)), dma((ny - 1,)),
        dma((nz - 1, 3)), dma((nz - 1, 3)),
        dma((2, 3)), dma((2, 3)),
    ]
    spec = pl.BlockSpec(memory_space=pltpu.VMEM)
    hbm = pl.BlockSpec(memory_space=pltpu.HBM)
    operands = [template, target, shifts, jnp.asarray(hart_hi), jnp.asarray(hart_lo),
                *map(jnp.asarray, (tables, hops, fold_hi, fold_lo, spread_hi, spread_lo, taps)),
                fractions]
    held = [vmem(x.shape, x.dtype) for x in operands[:-1]] + [pltpu.SMEM(fractions.shape, f32)]
    scratch = held + [dma((len(operands),)), dma((steps,))] + scratch
    return tuple(pl.pallas_call(
        functools.partial(kernel, ny, nz),
        out_shape=(vmem((3, depth, rows, width), f32), vmem((depth, rows, width), f32)),
        in_specs=[hbm] * len(operands),
        out_specs=(spec, spec),
        scratch_shapes=scratch,
        compiler_params=pltpu.CompilerParams(
            collective_id=0, has_side_effects=True),
    )(*operands))


def solution(mesh):
    return jax.shard_map(
        functools.partial(on_device, ny=mesh.shape["gy"], nz=mesh.shape["gz"]),
        mesh=mesh,
        in_specs=(P("gz", "gy", None), P("gz", "gy", None), P(None, None, "gz", "gy", None), P()),
        out_specs=(P(None, "gz", "gy", None), P("gz", "gy", None)),
        check_vma=False,
    )
```
